256 devices in a mesh: expert: 32 (over y, z_lo, x), replica: 8 (over z_hi, core).
Axes of the slice: x: 4, y: 4, z: 8 (z_hi: 4, z_lo: 2; z = z_hi * 2 + z_lo), core: 2. Of those that a mesh axis runs over, the one named last changes fastest.
Arguments:
- tokens: bfloat16 [4096, 4096], P('expert', 'replica'), may hold values from -6 to 6
- out_grad: bfloat16 [4096, 4096], P('expert', 'replica'), may hold values from -6 to 6
- expert_ids: int32 [4096, 8], P('expert'), may hold values from 0 to 63, all different within a row; in each aligned block of 128 rows (0 to 127, 128 to 255, ...) at most 20 rows name the same one
- route_weight: float32 [4096, 8], P('expert'), may hold values from 0.05 to 0.3
- gate_weight: bfloat16 [64, 4096, 768], P('expert', 'replica'), may hold values from -0.09375 to 0.09375
- up_weight: bfloat16 [64, 4096, 768], P('expert', 'replica'), may hold values from -0.09375 to 0.09375
- down_weight: bfloat16 [64, 768, 4096], P('expert', None, 'replica'), may hold values from -0.21875 to 0.21875
Outputs:
- mixed: bfloat16 [4096, 4096], P('expert', 'replica')
- in_grad: bfloat16 [4096, 4096], P('expert', 'replica')
- grad_gate: bfloat16 [64, 4096, 768], P('expert', 'replica')
- grad_up: bfloat16 [64, 4096, 768], P('expert', 'replica')
- grad_down: bfloat16 [64, 768, 4096], P('expert', None, 'replica')
The draws below stay inside these ranges and needn't reach their ends.
Inputs may be any that keep to these rules, and one draw needn't show every extreme that they name: `expert_ids`: each token names 8 different experts. Within the 128 rows of one index of expert no expert is named more than 20 times, a bound that some block reaches.
All inputs are finite; a program needn't handle non-finite values.
Results may differ from the reference program's by a relative error of at most 0.0064.
Values may be sent and summed in bfloat16 or wider, within the bound.
No kernel may reach another device: no remote copies, remote signals or barrier semaphores. Data moves between devices by JAX's collectives and lax.ppermute only.
A program may use at most 128 MiB of HBM per device.

```python
import math
import jax
import jax.numpy as jnp
import numpy as np
from jax import lax

D = 4096
H = 768
TOPK = 8
TOK_DEV = 128
EXPERTS = 64
CAP = 20
TOKENS = 4096
N_EXPERT = 32


def level_of(key, dims, cuts, least, high):
    factor_of, own = 1.0, jax.random.fold_in(key, 6)
    for axis_at, shards_of in cuts:
        heights = jnp.exp(jax.random.uniform(jax.random.fold_in(own, axis_at), (shards_of,), jnp.float32, least / len(cuts), high / len(cuts)))
        factor_of = factor_of * jnp.repeat(heights, dims[axis_at] // shards_of).reshape([-1 if axis == axis_at else 1 for axis in range(len(dims))])
    return factor_of


def routed_block(rng, own, number, rows, count, top, most, lean):
    order = jax.random.permutation(rng, count)
    crowded, usual = load_shares(count, rows * top, most, lean, True), load_shares(count, rows * top, most, lean, False)
    places = jnp.arange(count)

    def named(tallies, offset_by):
        used = int((tallies > 0).sum())
        fixed = max(1, used // 4)
        passed = fixed + (places - fixed + offset_by * (used - fixed)) % max(1, count - fixed)
        return jnp.zeros((count,), jnp.int32).at[order[jnp.where(places < fixed, places, passed)]].set(jnp.asarray(tallies, jnp.int32))

    tallies = jnp.where(number % 4 == 0, named(crowded, number // 4), named(usual, number - number // 4 - 1))
    mixed = jax.random.permutation(jax.random.fold_in(own, 3), count)
    source_of, sink = mixed[0:count // 2 * 2:2], mixed[1:count // 2 * 2:2]
    slack = jnp.minimum(tallies[source_of] - 1, most - tallies[sink]) // 2
    slack = jnp.where((source_of == order[0]) | (sink == order[0]) | (tallies[sink] == 0), 0, jnp.maximum(slack, 0))
    passed = jax.random.randint(jax.random.fold_in(own, 4), (count // 2,), 0, 1 << 20) % (slack + 1)
    tallies = tallies.at[source_of].add(-passed).at[sink].add(passed)
    items = jnp.searchsorted(jnp.cumsum(tallies), jnp.arange(rows * top), side="right").astype(jnp.int32)
    listing = items.reshape(top, rows).T
    listing = listing[jax.random.permutation(jax.random.fold_in(own, 1), rows)]
    offset_by = jax.random.randint(jax.random.fold_in(own, 2), (rows, 1), 0, top)
    return jnp.take_along_axis(listing, (jnp.arange(top)[None, :] + offset_by) % top, axis=1)


def load_shares(amount, total, limit, lean, full):
    loads = [(1 << 20) // math.isqrt(grade ** lean) + 1 for grade in range(1, amount + 1)]
    largest = limit if full else min(limit, max(-(-total // amount), total * loads[0] // sum(loads)))
    least = 1 if total - largest >= amount - 1 else 0
    given, surplus = [largest] + [least] * (amount - 1), total - largest - least * (amount - 1)
    while surplus > 0:
        movable = [i for i in range(1, amount) if given[i] < largest] or [i for i in range(1, amount) if given[i] < limit]
        whole, budget = sum([loads[i] for i in movable]), surplus
        for i in movable:
            more = min(limit - given[i], max(1, budget * loads[i] // whole), surplus)
            given[i] = given[i] + more
            surplus = surplus - more
    return np.array(given)


def noise(key, shape, deviation, bound, shards=(), kind=jnp.bfloat16):
    values = deviation * jax.random.normal(key, shape, jnp.float32)
    if shards:
        values = values * level_of(key, shape, shards, -0.22, 0.18)
    return jnp.clip(values, -bound, bound).astype(kind)


def setup_inputs(seed: int = 0) -> dict:
    splits = jax.random.split(jax.random.key(seed), 8)
    tokens = noise(splits[0], (TOKENS, D), 1.0, 6.0, ((0, 32), (1, 8)))
    out_grad = noise(splits[1], (TOKENS, D), 1.0, 6.0, ((0, 32), (1, 8)))
    expert_ids_keys = jax.random.split(jax.random.fold_in(splits[2], 1), TOKENS // TOK_DEV)
    expert_ids_turns = jax.random.permutation(jax.random.fold_in(splits[2], 3), TOKENS // TOK_DEV)
    expert_ids = jax.vmap(lambda own, number: routed_block(jax.random.fold_in(splits[2], 2), own, number, TOK_DEV, EXPERTS, TOPK, CAP, 2))(expert_ids_keys, expert_ids_turns).reshape((TOKENS, TOPK))
    route_weight = jnp.clip(0.05 + 0.25 * jax.random.uniform(splits[3], (TOKENS, TOPK), jnp.float32) ** level_of(splits[3], (TOKENS, TOPK), ((0, 32),), -0.2, 0.2), 0.05, 0.3)
    gate_weight = noise(splits[4], (EXPERTS, D, H), D ** -0.5, 0.09375, ((0, 32), (1, 8)))
    up_weight = noise(splits[5], (EXPERTS, D, H), D ** -0.5, 0.09375, ((0, 32), (1, 8)))
    down_weight = noise(splits[6], (EXPERTS, H, D), H ** -0.5, 0.21875, ((0, 32), (2, 8)))
    return {"tokens": tokens, "out_grad": out_grad, "expert_ids": expert_ids, "route_weight": route_weight, "gate_weight": gate_weight, "up_weight": up_weight, "down_weight": down_weight}


def reference(tokens, out_grad, expert_ids, route_weight, gate_weight, up_weight, down_weight):
    total = tokens.shape[0]
    flat_ids = expert_ids.reshape(N_EXPERT, TOK_DEV * TOPK)
    onehot = (flat_ids[:, :, None] == jnp.arange(EXPERTS, dtype=jnp.int32)[None, None, :]).astype(jnp.int32)
    ranks = jnp.sum((jnp.cumsum(onehot, axis=1) - 1) * onehot, axis=2).astype(jnp.int32)
    column = jnp.broadcast_to(jnp.arange(N_EXPERT, dtype=jnp.int32)[:, None], ranks.shape)
    token_of = (jnp.arange(total * TOPK, dtype=jnp.int32) // TOPK).reshape(N_EXPERT, TOK_DEV * TOPK)
    table = jnp.full((EXPERTS, N_EXPERT, CAP), total, jnp.int32)
    table = table.at[flat_ids, column, ranks].set(token_of)
    wtable = jnp.zeros((EXPERTS, N_EXPERT, CAP), jnp.float32)
    wtable = wtable.at[flat_ids, column, ranks].set(route_weight.reshape(N_EXPERT, TOK_DEV * TOPK).astype(jnp.float32))
    padded_x = jnp.concatenate([tokens, jnp.zeros((1, D), tokens.dtype)], axis=0)
    padded_dy = jnp.concatenate([out_grad.astype(jnp.float32), jnp.zeros((1, D), jnp.float32)], axis=0)

    def step(carry, item):
        out_acc, in_acc = carry
        rows, weights, w_gate, w_up, w_down = item
        rows = rows.reshape(-1)
        weights = weights.reshape(-1)
        slot_x = padded_x[rows]
        slot_g = (weights[:, None] * padded_dy[rows]).astype(jnp.bfloat16)
        gate = jnp.dot(slot_x, w_gate, preferred_element_type=jnp.float32)
        up = jnp.dot(slot_x, w_up, preferred_element_type=jnp.float32)
        sig = jax.nn.sigmoid(gate)
        act = gate * sig
        hidden = (act * up).astype(jnp.bfloat16)
        expert_out = jnp.dot(hidden, w_down, preferred_element_type=jnp.float32).astype(jnp.bfloat16)
        g_down = jnp.dot(hidden.T, slot_g, preferred_element_type=jnp.float32).astype(jnp.bfloat16)
        hidden_grad = jnp.dot(slot_g, w_down.T, preferred_element_type=jnp.float32)
        gate_grad = (hidden_grad * up * sig * (1.0 + gate * (1.0 - sig))).astype(jnp.bfloat16)
        up_grad = (hidden_grad * act).astype(jnp.bfloat16)
        g_gate = jnp.dot(slot_x.T, gate_grad, preferred_element_type=jnp.float32).astype(jnp.bfloat16)
        g_up = jnp.dot(slot_x.T, up_grad, preferred_element_type=jnp.float32).astype(jnp.bfloat16)
        slot_in = (jnp.dot(gate_grad, w_gate.T, preferred_element_type=jnp.float32)
                   + jnp.dot(up_grad, w_up.T, preferred_element_type=jnp.float32)).astype(jnp.bfloat16)
        out_acc = out_acc.at[rows].add(weights[:, None] * expert_out.astype(jnp.float32), mode="drop")
        in_acc = in_acc.at[rows].add(slot_in.astype(jnp.float32), mode="drop")
        return (out_acc, in_acc), (g_gate, g_up, g_down)

    start = (jnp.zeros((total, D), jnp.float32), jnp.zeros((total, D), jnp.float32))
    (out_acc, in_acc), (grad_gate, grad_up, grad_down) = lax.scan(
        step, start, (table, wtable, gate_weight, up_weight, down_weight))
    return (out_acc.astype(jnp.bfloat16), in_acc.astype(jnp.bfloat16), grad_gate, grad_up, grad_down)
```

```python
import jax
import jax.numpy as jnp
from jax import lax
from jax.sharding import PartitionSpec as P

F32 = jnp.float32
BF16 = jnp.bfloat16
CORES = 2


def dot(a, b, ca, cb):
    return lax.dot_general(a, b, (((ca,), (cb,)), ((), ())), preferred_element_type=F32)


def split3(w):
    hi = w.astype(BF16)
    rest = w - hi.astype(F32)
    mid = rest.astype(BF16)
    low = (rest - mid.astype(F32)).astype(BF16)
    return hi, mid, low


def local(tokens, out_grad, expert_ids, route_weight, gate_weight, up_weight, down_weight):
    n_cols = lax.axis_size("expert")
    n_reps = lax.axis_size("replica")
    tok_count, topk = expert_ids.shape
    local_experts, feats, width = gate_weight.shape
    experts_all = local_experts * n_cols
    cap = tok_count * topk * 5 // (4 * experts_all)
    slots = experts_all * cap
    chips = n_reps // CORES
    rows = slots // n_reps

    rep = lax.axis_index("replica")
    chip = rep // CORES
    core = rep % CORES
    step_of = 1 - 2 * core
    swap = [(r, r ^ 1) for r in range(n_reps)]
    ring = []
    for r in range(n_reps):
        c, k = r // CORES, r % CORES
        ring.append((r, (c + (1 if k == 0 else chips - 1)) % chips * CORES + k))

    def chunk(a, away):
        at = (chip - step_of * away + 2 * chips) % chips
        return lax.dynamic_index_in_dim(a, at, 0, keepdims=False)

    def reduce_scatter(part):
        cols = part.shape[1]
        part = part.reshape(CORES, chips * rows, cols)
        give = lax.dynamic_index_in_dim(part, 1 - core, 0, keepdims=False).astype(BF16)
        keep = lax.dynamic_index_in_dim(part, core, 0, keepdims=False)
        got = lax.ppermute(give, "replica", swap)
        both = (keep + got.astype(F32)).reshape(chips, rows, cols)
        acc = chunk(both, 1)
        for s in range(chips - 1):
            got = lax.ppermute(acc.astype(BF16), "replica", ring)
            acc = chunk(both, 2 + s) + got.astype(F32)
        return acc

    def all_gather(own):
        cols = own.shape[1]
        out = jnp.zeros((CORES, chips, rows, cols), BF16)
        cur = own
        for s in range(chips):
            if s > 0:
                cur = lax.ppermute(cur, "replica", ring)
            other = lax.ppermute(cur, "replica", swap)
            at = (chip - step_of * s + 2 * chips) % chips
            at_other = (chip + step_of * s + 2 * chips) % chips
            out = lax.dynamic_update_slice(out, cur[None, None], (core, at, 0, 0))
            out = lax.dynamic_update_slice(out, other[None, None], (1 - core, at_other, 0, 0))
        return out.reshape(slots, cols)

    experts = jnp.arange(experts_all, dtype=jnp.int32)
    hit = expert_ids[:, :, None] == experts[None, None, :]
    member = jnp.any(hit, axis=1)
    weight_te = jnp.sum(jnp.where(hit, route_weight[:, :, None], 0.0), axis=1)
    t_row = lax.broadcasted_iota(jnp.int32, (tok_count, tok_count), 0)
    t_col = lax.broadcasted_iota(jnp.int32, (tok_count, tok_count), 1)
    earlier = (t_col <= t_row).astype(BF16)
    rank1 = jnp.where(member, dot(earlier, member.astype(BF16), 1, 0), 0.0)
    slot = jnp.arange(slots, dtype=jnp.int32)
    spread = (experts[:, None] == slot[None, :] // cap).astype(BF16)
    rank1_s = dot(rank1.astype(BF16), spread, 1, 0)
    taken = rank1_s == (slot % cap + 1).astype(F32)[None, :]
    w_parts = split3(weight_te)
    weight_s = sum(dot(part, spread, 1, 0) for part in w_parts)
    weight_s = jnp.where(taken, weight_s, 0.0)
    picker = taken.astype(BF16)
    slot_weight = jnp.sum(weight_s, axis=0)

    send_x = dot(picker, tokens, 0, 0).astype(BF16)
    send_g = (slot_weight[:, None] * dot(picker, out_grad, 0, 0)).astype(BF16)

    def exchange(a):
        a = a.reshape(n_cols, local_experts * cap, feats)
        return lax.all_to_all(a, "expert", split_axis=0, concat_axis=0, tiled=True).reshape(slots, feats)

    recv_x = exchange(send_x)
    recv_g = exchange(send_g)

    expert_of = slot[:, None] // cap % local_experts

    def by_expert(a):
        masked = [jnp.where(expert_of == e, a, jnp.zeros((), a.dtype)) for e in range(local_experts)]
        return jnp.concatenate(masked, axis=1)

    x_by = by_expert(recv_x)
    gate_part = dot(x_by, gate_weight.reshape(-1, width), 1, 0)
    up_part = dot(x_by, up_weight.reshape(-1, width), 1, 0)
    gate_up = reduce_scatter(jnp.concatenate([gate_part, up_part], axis=1))
    hg_part = 0.0
    for e in range(local_experts):
        hg_part = jnp.where(expert_of == e, dot(recv_g, down_weight[e], 1, 1), hg_part)
    hidden_grad = reduce_scatter(hg_part)

    gate, up = gate_up[:, :width], gate_up[:, width:]
    sig = jax.nn.sigmoid(gate)
    act = gate * sig
    hidden = all_gather((act * up).astype(BF16))
    gate_grad = (hidden_grad * up * sig * (1.0 + gate * (1.0 - sig))).astype(BF16)
    up_grad = (hidden_grad * act).astype(BF16)
    grads = all_gather(jnp.concatenate([gate_grad, up_grad], axis=1))

    hidden_by = by_expert(hidden)
    expert_out = dot(hidden_by, down_weight.reshape(-1, feats), 1, 0).astype(BF16)
    returned = exchange(expert_out)
    mixed = sum(dot(part, returned, 1, 0) for part in split3(weight_s)).astype(BF16)
    grad_down = dot(hidden_by, recv_g, 0, 0).astype(BF16).reshape(down_weight.shape)

    gate_grad, up_grad = grads[:, :width], grads[:, width:]
    slot_in = 0.0
    for e in range(local_experts):
        mine = dot(gate_grad, gate_weight[e], 1, 1) + dot(up_grad, up_weight[e], 1, 1)
        slot_in = jnp.where(expert_of == e, mine, slot_in)
    back_in = exchange(slot_in.astype(BF16))
    in_grad = dot(picker, back_in, 1, 0).astype(BF16)
    grad_gate = dot(x_by, gate_grad, 0, 0).astype(BF16).reshape(gate_weight.shape)
    grad_up = dot(x_by, up_grad, 0, 0).astype(BF16).reshape(up_weight.shape)
    return (mixed, in_grad, grad_gate, grad_up, grad_down)


def solution(mesh):
    in_specs = (
        P("expert", "replica"),
        P("expert", "replica"),
        P("expert", None),
        P("expert", None),
        P("expert", "replica", None),
        P("expert", "replica", None),
        P("expert", None, "replica"),
    )
    out_specs = (
        P("expert", "replica"),
        P("expert", "replica"),
        P("expert", "replica", None),
        P("expert", "replica", None),
        P("expert", None, "replica"),
    )
    return jax.shard_map(local, mesh=mesh, in_specs=in_specs, out_specs=out_specs, check_vma=False)
```

```python
import functools
import jax
import jax.numpy as jnp
from jax import lax
from jax.experimental import pallas as pl
from jax.experimental.pallas import tpu as pltpu
from jax.sharding import PartitionSpec as P

F32 = jnp.float32
BF16 = jnp.bfloat16
CORES = 2


def dot(a, b, ca, cb):
    return lax.dot_general(a, b, (((ca,), (cb,)), ((), ())), preferred_element_type=F32)


def split3(w):
    hi = w.astype(BF16)
    rest = w - hi.astype(F32)
    mid = rest.astype(BF16)
    low = (rest - mid.astype(F32)).astype(BF16)
    return hi, mid, low


def expert_mask(rows, cap, experts, e):
    row = lax.broadcasted_iota(jnp.int32, (rows, 1), 0)
    return row // cap % experts == e


def chunk_rows(where, away, chips, rows):
    return pl.ds(pl.multiple_of((where[0] + away) % chips * rows, 16), rows)


def gate_up_kernel(cap, where, x_ref, other_ref, gm, go, um, uo, up_ref, down_ref, keep_ref, own_ref, x_by, acc):
    experts, feats, _ = gm.shape
    half = other_ref.shape[0]
    rows = own_ref.shape[1]
    chips = half // rows

    @pl.when(pl.program_id(0) == 0)
    def _():
        mine = x_ref[pl.ds(pl.multiple_of(where[1] * half, 16), half), :]
        other = other_ref[...]
        for e in range(experts):
            mask = expert_mask(half, cap, experts, e)
            x_by[e] = jnp.where(mask, mine, jnp.zeros_like(mine))
            x_by[experts + e] = jnp.where(mask, other, jnp.zeros_like(other))

    for i, (wm, wo) in enumerate(((gm, go), (um, uo))):
        total = dot(x_by[0], wm[0], 1, 0)
        for e in range(1, experts):
            total += dot(x_by[e], wm[e], 1, 0)
        for e in range(experts):
            total += dot(x_by[experts + e], wo[e], 1, 0)
        acc[i] = total
    at = functools.partial(chunk_rows, where, chips=chips, rows=rows)
    up_ref[0] = acc[0, at(2), :].astype(BF16)
    up_ref[1] = acc[1, at(1), :].astype(BF16)
    down_ref[0] = acc[1, at(2), :].astype(BF16)
    down_ref[1] = acc[0, at(chips - 1), :].astype(BF16)
    keep_ref[0] = acc[0, at(1), :]
    keep_ref[1] = acc[1, at(chips - 1), :]
    own_ref[0] = acc[0, at(0), :]
    own_ref[1] = acc[1, at(0), :]


def gate_up(where, x, other, gm, go, um, uo, cap, rows):
    experts, feats, width = gm.shape
    half = other.shape[0]
    tile = 256
    weight = pl.BlockSpec((experts, feats, tile), lambda n, w: (0, 0, n))
    out = pl.BlockSpec((2, rows, tile), lambda n, w: (0, 0, n))
    shape = (2, rows, width)
    return pl.pallas_call(
        functools.partial(gate_up_kernel, cap),
        grid_spec=pltpu.PrefetchScalarGridSpec(
            num_scalar_prefetch=1,
            grid=(width // tile,),
            in_specs=[
                pl.BlockSpec(x.shape, lambda n, w: (0, 0)),
                pl.BlockSpec(other.shape, lambda n, w: (0, 0)),
                weight, weight, weight, weight,
            ],
            out_specs=[out, out, out, out],
            scratch_shapes=[
                pltpu.VMEM((2 * experts, half, feats), BF16),
                pltpu.VMEM((2, half, tile), F32),
            ],
        ),
        out_shape=[
            jax.ShapeDtypeStruct(shape, BF16),
            jax.ShapeDtypeStruct(shape, BF16),
            jax.ShapeDtypeStruct(shape, F32),
            jax.ShapeDtypeStruct(shape, F32),
        ],
        name="gate_up",
    )(where, x, other, gm, go, um, uo)


def hidden_grad_kernel(cap, where, g_ref, other_ref, dm, do, up_ref, down_ref, keep_ref, own_ref, acc):
    experts = dm.shape[0]
    half = other_ref.shape[0]
    part = own_ref.shape[1]
    rows = 2 * part
    chips = half // rows
    mine = g_ref[pl.ds(pl.multiple_of(where[1] * half, 16), half), :]
    other = other_ref[...]
    total = None
    for e in range(experts):
        one = dot(mine, dm[e], 1, 1) + dot(other, do[e], 1, 1)
        total = one if e == 0 else jnp.where(expert_mask(half, cap, experts, e), one, total)
    acc[...] = total

    def at(away, k):
        start = (where[0] + away) % chips * rows + k * part
        return acc[pl.ds(pl.multiple_of(start, 16), part), :]

    up_ref[0] = at(2, 0).astype(BF16)
    up_ref[1] = at(1, 1).astype(BF16)
    down_ref[0] = at(2, 1).astype(BF16)
    down_ref[1] = at(chips - 1, 0).astype(BF16)
    keep_ref[0] = at(1, 0)
    keep_ref[1] = at(chips - 1, 1)
    own_ref[0] = at(0, 0)
    own_ref[1] = at(0, 1)


def hidden_grad_parts(where, g, other, dm, do, cap, rows):
    experts, width, feats = dm.shape
    half = other.shape[0]
    tile = 256
    weight = pl.BlockSpec((experts, tile, feats), lambda n, w: (0, n, 0))
    out = pl.BlockSpec((2, rows // 2, tile), lambda n, w: (0, 0, n))
    shape = (2, rows // 2, width)
    return pl.pallas_call(
        functools.partial(hidden_grad_kernel, cap),
        grid_spec=pltpu.PrefetchScalarGridSpec(
            num_scalar_prefetch=1,
            grid=(width // tile,),
            in_specs=[
                pl.BlockSpec(g.shape, lambda n, w: (0, 0)),
                pl.BlockSpec(other.shape, lambda n, w: (0, 0)),
                weight, weight,
            ],
            out_specs=[out, out, out, out],
            scratch_shapes=[pltpu.VMEM((half, tile), F32)],
        ),
        out_shape=[
            jax.ShapeDtypeStruct(shape, BF16),
            jax.ShapeDtypeStruct(shape, BF16),
            jax.ShapeDtypeStruct(shape, F32),
            jax.ShapeDtypeStruct(shape, F32),
        ],
        name="hidden_grad",
    )(where, g, other, dm, do)


def gather_rows(where, out, pieces, chips, rows):
    half = chips * rows
    for k, (own, low, high, far_a, far_b) in enumerate(pieces):
        core = where[1] if k == 0 else 1 - where[1]

        def put(away, value, skip=0):
            start = core * half + (where[0] + away) % chips * rows + skip
            out[pl.ds(pl.multiple_of(start, 16), value.shape[0]), :] = value

        put(0, own[...])
        put(chips - 1, low[...])
        put(1, high[...])
        put(2, far_a[...])
        if far_b is not None:
            put(2, far_b[...], far_a.shape[0])


def expert_out_kernel(cap, chips, where, *refs):
    pieces, (weight, out_ref, all_ref) = refs[:10], refs[10:]
    experts, width, feats = weight.shape
    rows = pieces[0].shape[0]
    gather_rows(where, all_ref, (pieces[:5], pieces[5:]), chips, rows)
    total = None
    for e in range(experts):
        one = dot(all_ref[...], weight[e], 1, 0)
        total = one if e == 0 else jnp.where(expert_mask(one.shape[0], cap, experts, e), one, total)
    out_ref[...] = total.astype(BF16)


def expert_out_of(where, pieces, weight, cap, chips):
    experts, width, feats = weight.shape
    slots = CORES * chips * pieces[0].shape[0]
    vmem = pl.BlockSpec(memory_space=pltpu.VMEM)
    return pl.pallas_call(
        functools.partial(expert_out_kernel, cap, chips),
        in_specs=[pl.BlockSpec(memory_space=pltpu.SMEM)] + [vmem] * 11,
        out_specs=[vmem, vmem],
        out_shape=[
            jax.ShapeDtypeStruct((slots, feats), BF16),
            jax.ShapeDtypeStruct((slots, width), BF16),
        ],
        name="expert_out",
    )(where, *pieces, weight)


def slot_in_kernel(cap, chips, where, *refs):
    own, low, high, far_g, far_u, own2, low2, high2, far_g2, far_u2, gw, uw, out_ref, gate_ref, up_ref = refs
    experts = gw.shape[0]
    rows = own.shape[1]
    for i, ref in enumerate((gate_ref, up_ref)):
        first = (own.at[i], low.at[i], high.at[i], (far_g, far_u)[i], None)
        second = (own2.at[i], low2.at[i], high2.at[i], (far_g2, far_u2)[i], None)
        gather_rows(where, ref, (first, second), chips, rows)
    total = None
    for e in range(experts):
        one = dot(gate_ref[...], gw[e], 1, 1) + dot(up_ref[...], uw[e], 1, 1)
        total = one if e == 0 else jnp.where(expert_mask(one.shape[0], cap, experts, e), one, total)
    out_ref[...] = total.astype(BF16)


def slot_in_of(where, pieces, gw, uw, cap, chips):
    experts, feats, width = gw.shape
    slots = CORES * chips * pieces[0].shape[1]
    vmem = pl.BlockSpec(memory_space=pltpu.VMEM)
    return pl.pallas_call(
        functools.partial(slot_in_kernel, cap, chips),
        in_specs=[pl.BlockSpec(memory_space=pltpu.SMEM)] + [vmem] * 12,
        out_specs=[vmem] * 3,
        out_shape=[
            jax.ShapeDtypeStruct((slots, feats), BF16),
            jax.ShapeDtypeStruct((slots, width), BF16),
            jax.ShapeDtypeStruct((slots, width), BF16),
        ],
        name="slot_in",
    )(where, *pieces, gw, uw)


def local(tokens, out_grad, expert_ids, route_weight, gate_weight, up_weight, down_weight):
    n_cols = lax.axis_size("expert")
    n_reps = lax.axis_size("replica")
    tok_count, topk = expert_ids.shape
    local_experts, feats, width = gate_weight.shape
    experts_all = local_experts * n_cols
    cap = tok_count * topk * 5 // (4 * experts_all)
    slots = experts_all * cap
    chips = n_reps // CORES
    rows = slots // n_reps
    half = slots // CORES

    rep = lax.axis_index("replica")
    core = rep % CORES
    where = jnp.stack([rep // CORES, core]).astype(jnp.int32)
    to_swap = [(r, r ^ 1) for r in range(n_reps)]
    to_up = [(r, (r + CORES) % n_reps) for r in range(n_reps)]
    to_down = [(r, (r - CORES) % n_reps) for r in range(n_reps)]

    def swap(a):
        return lax.ppermute(a, "replica", to_swap)

    def up_one(a):
        return lax.ppermute(a, "replica", to_up)

    def down_one(a):
        return lax.ppermute(a, "replica", to_down)

    def tree_sum(send_up, send_down, keep, own):
        low = up_one(send_up)
        high = down_one(send_down)
        first = up_one((keep[0] + low[0].astype(F32)).astype(BF16))
        second = down_one((keep[1] + high[0].astype(F32)).astype(BF16))
        a = own[0] + high[1].astype(F32) + first.astype(F32)
        b = own[1] + low[1].astype(F32) + second.astype(F32)
        return a, b

    gate_other = swap(gate_weight)
    up_other = swap(up_weight)
    down_other = swap(down_weight)

    experts = jnp.arange(experts_all, dtype=jnp.int32)
    hit = expert_ids[:, :, None] == experts[None, None, :]
    member = jnp.any(hit, axis=1)
    weight_te = jnp.sum(jnp.where(hit, route_weight[:, :, None], 0.0), axis=1)
    t_row = lax.broadcasted_iota(jnp.int32, (tok_count, tok_count), 0)
    t_col = lax.broadcasted_iota(jnp.int32, (tok_count, tok_count), 1)
    earlier = (t_col <= t_row).astype(BF16)
    rank1 = jnp.where(member, dot(earlier, member.astype(BF16), 1, 0), 0.0)
    slot = jnp.arange(slots, dtype=jnp.int32)
    spread = (experts[:, None] == slot[None, :] // cap).astype(BF16)
    rank1_s = dot(rank1.astype(BF16), spread, 1, 0)
    taken = rank1_s == (slot % cap + 1).astype(F32)[None, :]
    weight_s = sum(dot(part, spread, 1, 0) for part in split3(weight_te))
    weight_s = jnp.where(taken, weight_s, 0.0)
    picker = taken.astype(BF16)
    slot_weight = jnp.sum(weight_s, axis=0)

    send_x = dot(picker, tokens, 0, 0).astype(BF16)
    send_g = (slot_weight[:, None] * dot(picker, out_grad, 0, 0)).astype(BF16)

    def exchange(a):
        a = a.reshape(n_cols, local_experts * cap, feats)
        return lax.all_to_all(a, "expert", split_axis=0, concat_axis=0, tiled=True).reshape(slots, feats)

    def other_half(a):
        return swap(lax.dynamic_slice_in_dim(a, (1 - core) * half, half, 0))

    recv_x = exchange(send_x)
    recv_g = exchange(send_g)
    gate, up = tree_sum(*gate_up(
        where, recv_x, other_half(recv_x), gate_weight, gate_other, up_weight, up_other, cap, rows))
    grad_a, grad_b = tree_sum(*hidden_grad_parts(
        where, recv_g, other_half(recv_g), down_weight, down_other, cap, rows))
    hidden_grad = jnp.concatenate([grad_a, grad_b], axis=0)

    sig = jax.nn.sigmoid(gate)
    act = gate * sig
    own = (act * up).astype(BF16)
    low, high = up_one(own), down_one(own)
    far_a, far_b = up_one(low[:rows // 2]), down_one(high[rows // 2:])
    pieces = [own, low, high, far_a, far_b]
    pieces = pieces + [swap(a) for a in pieces]
    expert_out, hidden = expert_out_of(where, pieces, down_weight, cap, chips)
    returned = exchange(expert_out)
    mixed = sum(dot(part, returned, 1, 0) for part in split3(weight_s)).astype(BF16)

    gate_grad = (hidden_grad * up * sig * (1.0 + gate * (1.0 - sig))).astype(BF16)
    up_grad = (hidden_grad * act).astype(BF16)
    own = jnp.stack([gate_grad, up_grad])
    low, high = up_one(own), down_one(own)
    far_g, far_u = up_one(low[0]), down_one(high[1])
    pieces = [own, low, high, far_g, far_u]
    pieces = pieces + [swap(a) for a in pieces]
    slot_in, gate_grad, up_grad = slot_in_of(where, pieces, gate_weight, up_weight, cap, chips)
    back_in = exchange(slot_in)
    in_grad = dot(picker, back_in, 1, 0).astype(BF16)

    expert_of = slot[:, None] // cap % local_experts

    def by_expert(a):
        masked = [jnp.where(expert_of == e, a, jnp.zeros((), a.dtype)) for e in range(local_experts)]
        return jnp.concatenate(masked, axis=1)

    x_by = by_expert(recv_x)
    grad_down = dot(by_expert(hidden), recv_g, 0, 0).astype(BF16).reshape(down_weight.shape)
    grad_gate = dot(x_by, gate_grad, 0, 0).astype(BF16).reshape(gate_weight.shape)
    grad_up = dot(x_by, up_grad, 0, 0).astype(BF16).reshape(up_weight.shape)
    return (mixed, in_grad, grad_gate, grad_up, grad_down)


def solution(mesh):
    in_specs = (
        P("expert", "replica"),
        P("expert", "replica"),
        P("expert", None),
        P("expert", None),
        P("expert", "replica", None),
        P("expert", "replica", None),
        P("expert", None, "replica"),
    )
    out_specs = (
        P("expert", "replica"),
        P("expert", "replica"),
        P("expert", "replica", None),
        P("expert", "replica", None),
        P("expert", None, "replica"),
    )
    return jax.shard_map(local, mesh=mesh, in_specs=in_specs, out_specs=out_specs, check_vma=False)
```

```python
import functools
import jax
import jax.numpy as jnp
from jax import lax
from jax.experimental import pallas as pl
from jax.experimental.pallas import tpu as pltpu
from jax.sharding import Mesh, PartitionSpec as P


F32 = jnp.float32
BF16 = jnp.bfloat16
CORES = 2


def dot(a, b, ca, cb):
    return lax.dot_general(a, b, (((ca,), (cb,)), ((), ())), preferred_element_type=F32)


def split3(w):
    hi = w.astype(BF16)
    rest = w - hi.astype(F32)
    mid = rest.astype(BF16)
    low = (rest - mid.astype(F32)).astype(BF16)
    return hi, mid, low


def expert_mask(rows, cap, experts, e):
    row = lax.broadcasted_iota(jnp.int32, (rows, 1), 0)
    return row // cap % experts == e


def chunk_rows(where, away, chips, rows):
    return pl.ds(pl.multiple_of((where[0] + away) % chips * rows, 16), rows)


def gate_up_kernel(cap, where, x_ref, other_ref, gm, go, um, uo, up_ref, down_ref, keep_ref, own_ref, x_by, acc):
    experts, _, _ = gm.shape
    half = other_ref.shape[0]
    rows = own_ref.shape[1]
    chips = half // rows

    @pl.when(pl.program_id(0) == 0)
    def _():
        mine = x_ref[pl.ds(pl.multiple_of(where[1] * half, 16), half), :]
        other = other_ref[...]
        for e in range(experts):
            mask = expert_mask(half, cap, experts, e)
            x_by[e] = jnp.where(mask, mine, jnp.zeros_like(mine))
            x_by[experts + e] = jnp.where(mask, other, jnp.zeros_like(other))

    for i, (wm, wo) in enumerate(((gm, go), (um, uo))):
        total = dot(x_by[0], wm[0], 1, 0)
        for e in range(1, experts):
            total += dot(x_by[e], wm[e], 1, 0)
        for e in range(experts):
            total += dot(x_by[experts + e], wo[e], 1, 0)
        acc[i] = total
    at = functools.partial(chunk_rows, where, chips=chips, rows=rows)
    up_ref[0] = acc[0, at(2), :].astype(BF16)
    up_ref[1] = acc[1, at(1), :].astype(BF16)
    down_ref[0] = acc[1, at(2), :].astype(BF16)
    down_ref[1] = acc[0, at(chips - 1), :].astype(BF16)
    keep_ref[0] = acc[0, at(1), :]
    keep_ref[1] = acc[1, at(chips - 1), :]
    own_ref[0] = acc[0, at(0), :]
    own_ref[1] = acc[1, at(0), :]


def gate_up(where, x, other, gm, go, um, uo, cap, rows):
    experts, feats, width = gm.shape
    half = other.shape[0]
    tile = 256
    weight = pl.BlockSpec((experts, feats, tile), lambda n, w: (0, 0, n))
    out = pl.BlockSpec((2, rows, tile), lambda n, w: (0, 0, n))
    shape = (2, rows, width)
    return pl.pallas_call(
        functools.partial(gate_up_kernel, cap),
        grid_spec=pltpu.PrefetchScalarGridSpec(
            num_scalar_prefetch=1,
            grid=(width // tile,),
            in_specs=[
                pl.BlockSpec(x.shape, lambda n, w: (0, 0)),
                pl.BlockSpec(other.shape, lambda n, w: (0, 0)),
                weight, weight, weight, weight,
            ],
            out_specs=[out, out, out, out],
            scratch_shapes=[
                pltpu.VMEM((2 * experts, half, feats), BF16),
                pltpu.VMEM((2, half, tile), F32),
            ],
        ),
        out_shape=[
            jax.ShapeDtypeStruct(shape, BF16),
            jax.ShapeDtypeStruct(shape, BF16),
            jax.ShapeDtypeStruct(shape, F32),
            jax.ShapeDtypeStruct(shape, F32),
        ],
        name="gate_up",
    )(where, x, other, gm, go, um, uo)


def hidden_grad_kernel(cap, where, g_ref, other_ref, dm, do, up_ref, down_ref, keep_ref, own_ref, acc):
    experts = dm.shape[0]
    half = other_ref.shape[0]
    part = own_ref.shape[1]
    rows = 2 * part
    chips = half // rows
    mine = g_ref[pl.ds(pl.multiple_of(where[1] * half, 16), half), :]
    other = other_ref[...]
    total = None
    for e in range(experts):
        one = dot(mine, dm[e], 1, 1) + dot(other, do[e], 1, 1)
        total = one if e == 0 else jnp.where(expert_mask(half, cap, experts, e), one, total)
    acc[...] = total

    def at(away, k):
        start = (where[0] + away) % chips * rows + k * part
        return acc[pl.ds(pl.multiple_of(start, 16), part), :]

    up_ref[0] = at(2, 0).astype(BF16)
    up_ref[1] = at(1, 1).astype(BF16)
    down_ref[0] = at(2, 1).astype(BF16)
    down_ref[1] = at(chips - 1, 0).astype(BF16)
    keep_ref[0] = at(1, 0)
    keep_ref[1] = at(chips - 1, 1)
    own_ref[0] = at(0, 0)
    own_ref[1] = at(0, 1)


def hidden_grad_parts(where, g, other, dm, do, cap, rows):
    experts, width, feats = dm.shape
    half = other.shape[0]
    tile = 256
    weight = pl.BlockSpec((experts, tile, feats), lambda n, w: (0, n, 0))
    out = pl.BlockSpec((2, rows // 2, tile), lambda n, w: (0, 0, n))
    shape = (2, rows // 2, width)
    return pl.pallas_call(
        functools.partial(hidden_grad_kernel, cap),
        grid_spec=pltpu.PrefetchScalarGridSpec(
            num_scalar_prefetch=1,
            grid=(width // tile,),
            in_specs=[
                pl.BlockSpec(g.shape, lambda n, w: (0, 0)),
                pl.BlockSpec(other.shape, lambda n, w: (0, 0)),
                weight, weight,
            ],
            out_specs=[out, out, out, out],
            scratch_shapes=[pltpu.VMEM((half, tile), F32)],
        ),
        out_shape=[
            jax.ShapeDtypeStruct(shape, BF16),
            jax.ShapeDtypeStruct(shape, BF16),
            jax.ShapeDtypeStruct(shape, F32),
            jax.ShapeDtypeStruct(shape, F32),
        ],
        name="hidden_grad",
    )(where, g, other, dm, do)


def gather_rows(where, out, pieces, chips, rows):
    half = chips * rows
    for k, (own, low, high, far_a, far_b) in enumerate(pieces):
        core = where[1] if k == 0 else 1 - where[1]

        def put(away, value, skip=0):
            start = core * half + (where[0] + away) % chips * rows + skip
            out[pl.ds(pl.multiple_of(start, 16), value.shape[0]), :] = value

        put(0, own[...])
        put(chips - 1, low[...])
        put(1, high[...])
        put(2, far_a[...])
        if far_b is not None:
            put(2, far_b[...], far_a.shape[0])


def expert_out_kernel(cap, chips, where, *refs):
    pieces, (weight, out_ref, all_ref) = refs[:10], refs[10:]
    experts, _, _ = weight.shape
    rows = pieces[0].shape[0]
    gather_rows(where, all_ref, (pieces[:5], pieces[5:]), chips, rows)
    total = None
    for e in range(experts):
        one = dot(all_ref[...], weight[e], 1, 0)
        total = one if e == 0 else jnp.where(expert_mask(one.shape[0], cap, experts, e), one, total)
    out_ref[...] = total.astype(BF16)


def expert_out_of(where, pieces, weight, cap, chips):
    _, width, feats = weight.shape
    slots = CORES * chips * pieces[0].shape[0]
    vmem = pl.BlockSpec(memory_space=pltpu.VMEM)
    return pl.pallas_call(
        functools.partial(expert_out_kernel, cap, chips),
        in_specs=[pl.BlockSpec(memory_space=pltpu.SMEM)] + [vmem] * 11,
        out_specs=[vmem, vmem],
        out_shape=[
            jax.ShapeDtypeStruct((slots, feats), BF16),
            jax.ShapeDtypeStruct((slots, width), BF16),
        ],
        name="expert_out",
    )(where, *pieces, weight)


def slot_in_kernel(cap, chips, where, *refs):
    own, low, high, far_g, far_u, own2, low2, high2, far_g2, far_u2, gw, uw, out_ref, gate_ref, up_ref = refs
    experts = gw.shape[0]
    rows = own.shape[1]
    for i, ref in enumerate((gate_ref, up_ref)):
        first = (own.at[i], low.at[i], high.at[i], (far_g, far_u)[i], None)
        second = (own2.at[i], low2.at[i], high2.at[i], (far_g2, far_u2)[i], None)
        gather_rows(where, ref, (first, second), chips, rows)
    total = None
    for e in range(experts):
        one = dot(gate_ref[...], gw[e], 1, 1) + dot(up_ref[...], uw[e], 1, 1)
        total = one if e == 0 else jnp.where(expert_mask(one.shape[0], cap, experts, e), one, total)
    out_ref[...] = total.astype(BF16)


def slot_in_of(where, pieces, gw, uw, cap, chips):
    _, feats, width = gw.shape
    slots = CORES * chips * pieces[0].shape[1]
    vmem = pl.BlockSpec(memory_space=pltpu.VMEM)
    return pl.pallas_call(
        functools.partial(slot_in_kernel, cap, chips),
        in_specs=[pl.BlockSpec(memory_space=pltpu.SMEM)] + [vmem] * 12,
        out_specs=[vmem] * 3,
        out_shape=[
            jax.ShapeDtypeStruct((slots, feats), BF16),
            jax.ShapeDtypeStruct((slots, width), BF16),
            jax.ShapeDtypeStruct((slots, width), BF16),
        ],
        name="slot_in",
    )(where, *pieces, gw, uw)


def routing(ids, weight, owner, allowed, block, experts_all, cap):
    rows = ids.shape[0]
    experts = jnp.arange(experts_all, dtype=jnp.int32)
    hit = ids[:, :, None] == experts[None, None, :]
    member = jnp.any(hit, axis=1)
    t_row = lax.broadcasted_iota(jnp.int32, (rows, rows), 0)
    t_col = lax.broadcasted_iota(jnp.int32, (rows, rows), 1)
    earlier = ((t_col <= t_row) & (t_col // block == t_row // block)).astype(BF16)
    rank1 = jnp.where(member, dot(earlier, member.astype(BF16), 1, 0), 0.0)
    slot = jnp.arange(owner.shape[0], dtype=jnp.int32)
    spread = (experts[:, None] == owner[None, :]).astype(BF16)
    rank1_s = dot(rank1.astype(BF16), spread, 1, 0)
    taken = rank1_s == (slot % cap + 1).astype(F32)[None, :]
    if allowed is not None:
        taken = taken & allowed
    if weight is None:
        return taken.astype(BF16)
    weight_te = jnp.sum(jnp.where(hit, weight[:, :, None], 0.0), axis=1)
    weight_s = sum(dot(part, spread, 1, 0) for part in split3(weight_te))
    return taken.astype(BF16), jnp.where(taken, weight_s, 0.0)


def weighted_sum(weight_s, rows):
    return sum(dot(part, rows, 1, 0) for part in split3(weight_s))


def layer(tokens, out_grad, expert_ids, route_weight, gate_weight, up_weight, down_weight):
    n_y, n_z, n_x = (lax.axis_size(a) for a in ("y", "z_lo", "x"))
    n_cols = n_y * n_z * n_x
    n_reps = lax.axis_size("replica")
    tok_count, topk = expert_ids.shape
    local_experts, feats, _ = gate_weight.shape
    experts_all = local_experts * n_cols
    cap = tok_count * topk * 5 // (4 * experts_all)
    slots = experts_all * cap
    chips = n_reps // CORES
    rows = slots // n_reps
    half = slots // CORES

    rep = lax.axis_index("replica")
    core = rep % CORES
    where = jnp.stack([rep // CORES, core]).astype(jnp.int32)
    to_swap = [(r, r ^ 1) for r in range(n_reps)]
    to_up = [(r, (r + CORES) % n_reps) for r in range(n_reps)]
    to_down = [(r, (r - CORES) % n_reps) for r in range(n_reps)]

    def swap(a):
        return lax.ppermute(a, "replica", to_swap)

    def up_one(a):
        return lax.ppermute(a, "replica", to_up)

    def down_one(a):
        return lax.ppermute(a, "replica", to_down)

    def tree_sum(send_up, send_down, keep, own):
        low = up_one(send_up)
        high = down_one(send_down)
        first = up_one((keep[0] + low[0].astype(F32)).astype(BF16))
        second = down_one((keep[1] + high[0].astype(F32)).astype(BF16))
        a = own[0] + high[1].astype(F32) + first.astype(F32)
        b = own[1] + low[1].astype(F32) + second.astype(F32)
        return a, b

    plane = n_y * n_x
    z_lo = lax.axis_index("z_lo")
    to_plane = [(z, n_z - 1 - z) for z in range(n_z)]

    def cross(a):
        return lax.ppermute(a, "z_lo", to_plane)

    gate_other = swap(gate_weight)
    up_other = swap(up_weight)
    down_other = swap(down_weight)

    block_rows = local_experts * cap

    def owner_of(y, x, z, inner):
        return ((y * n_z + z) * n_x + x) * local_experts + inner // cap

    slot = jnp.arange(slots, dtype=jnp.int32)
    at, inner = slot // block_rows, slot % block_rows
    owner = owner_of(at // n_z // n_x, at // n_z % n_x, at % n_z, inner)
    picker = routing(expert_ids, None, owner, None, tok_count, experts_all, cap)
    send_x = dot(picker, tokens, 0, 0).astype(BF16)

    def exchange(a):
        a = a.reshape(n_cols, block_rows, feats)
        return lax.all_to_all(a, ("y", "x", "z_lo"), split_axis=0, concat_axis=0, tiled=True).reshape(slots, feats)

    def exchange_plane(a):
        a = a.reshape(plane, n_z * block_rows, feats)
        return lax.all_to_all(a, ("y", "x"), split_axis=0, concat_axis=0, tiled=True).reshape(slots, feats)

    def other_half(a):
        return swap(lax.dynamic_slice_in_dim(a, (1 - core) * half, half, 0))

    ids_other = cross(expert_ids)
    weight_other = cross(route_weight)
    out_grad_other = cross(out_grad)

    recv_x = exchange(send_x)
    x_other = other_half(recv_x)
    sends = gate_up(where, recv_x, x_other, gate_weight, gate_other, up_weight, up_other, cap, rows)
    gate, up = tree_sum(*sends)

    def by_plane(mine, far):
        first = lax.select_n(z_lo == 0, far, mine)
        return jnp.concatenate([first, lax.select_n(z_lo == 0, mine, far)], axis=0)

    owner = owner_of(at // n_z // n_x, at // n_z % n_x, z_lo, inner)
    token = jnp.arange(n_z * tok_count, dtype=jnp.int32)
    same = token[:, None] // tok_count == at[None, :] % n_z
    picker2, weight2 = routing(
        by_plane(expert_ids, ids_other), by_plane(route_weight, weight_other),
        owner, same, tok_count, experts_all, cap)
    picked_g = dot(picker2, by_plane(out_grad, out_grad_other), 0, 0)
    send_g = (jnp.sum(weight2, axis=0)[:, None] * picked_g).astype(BF16)
    recv_g = exchange_plane(send_g)
    g_other = other_half(recv_g)
    grad_a, grad_b = tree_sum(*hidden_grad_parts(where, recv_g, g_other, down_weight, down_other, cap, rows))
    hidden_grad = jnp.concatenate([grad_a, grad_b], axis=0)

    sig = jax.nn.sigmoid(gate)
    act = gate * sig
    own = (act * up).astype(BF16)
    low, high = up_one(own), down_one(own)
    far_a, far_b = up_one(low[:rows // 2]), down_one(high[rows // 2:])
    pieces = [own, low, high, far_a, far_b]
    pieces = pieces + [swap(a) for a in pieces]
    expert_out, hidden = expert_out_of(where, pieces, down_weight, cap, chips)
    returned = exchange_plane(expert_out)
    sums = weighted_sum(weight2, returned).reshape(n_z, tok_count, feats)
    mine = lax.select_n(z_lo == 0, sums[1], sums[0])
    from_far = cross(lax.select_n(z_lo == 0, sums[0], sums[1]))
    mixed = (mine + from_far).astype(BF16)

    gate_grad = (hidden_grad * up * sig * (1.0 + gate * (1.0 - sig))).astype(BF16)
    up_grad = (hidden_grad * act).astype(BF16)
    own = jnp.stack([gate_grad, up_grad])
    low, high = up_one(own), down_one(own)
    far_g, far_u = up_one(low[0]), down_one(high[1])
    pieces = [own, low, high, far_g, far_u]
    pieces = pieces + [swap(a) for a in pieces]
    slot_in, gate_grad, up_grad = slot_in_of(where, pieces, gate_weight, up_weight, cap, chips)
    back_in = exchange(slot_in)
    in_grad = dot(picker, back_in, 1, 0).astype(BF16)

    expert_of = slot[:, None] // cap % local_experts

    def by_expert(a):
        masked = [jnp.where(expert_of == e, a, jnp.zeros((), a.dtype)) for e in range(local_experts)]
        return jnp.concatenate(masked, axis=1)

    x_by = by_expert(recv_x)
    grad_down = dot(by_expert(hidden), recv_g, 0, 0).astype(BF16).reshape(down_weight.shape)
    grad_gate = dot(x_by, gate_grad, 0, 0).astype(BF16).reshape(gate_weight.shape)
    grad_up = dot(x_by, up_grad, 0, 0).astype(BF16).reshape(up_weight.shape)
    return (mixed, in_grad, grad_gate, grad_up, grad_down)


def solution(mesh):
    n_y, n_z, n_x = 4, 2, 4
    devices = mesh.devices.reshape(n_y, n_z, n_x, mesh.shape["replica"])
    mesh = Mesh(devices, ("y", "z_lo", "x", "replica"))
    cols = ("y", "z_lo", "x")
    in_specs = (
        P(cols, "replica"),
        P(cols, "replica"),
        P(cols, None),
        P(cols, None),
        P(cols, "replica", None),
        P(cols, "replica", None),
        P(cols, None, "replica"),
    )
    out_specs = (
        P(cols, "replica"),
        P(cols, "replica"),
        P(cols, "replica", None),
        P(cols, "replica", None),
        P(cols, None, "replica"),
    )
    return jax.shard_map(layer, mesh=mesh, in_specs=in_specs, out_specs=out_specs, check_vma=False)
```

```python
import functools
import jax
import jax.numpy as jnp
from jax import lax
from jax.experimental import pallas as pl
from jax.experimental.pallas import tpu as pltpu
from jax.sharding import Mesh, PartitionSpec as P


F32 = jnp.float32
BF16 = jnp.bfloat16
CORES = 2


def dot(a, b, ca, cb):
    return lax.dot_general(a, b, (((ca,), (cb,)), ((), ())), preferred_element_type=F32)


def split3(w):
    hi = w.astype(BF16)
    rest = w - hi.astype(F32)
    mid = rest.astype(BF16)
    low = (rest - mid.astype(F32)).astype(BF16)
    return hi, mid, low


def chunk_rows(where, away, chips, rows):
    return pl.ds(pl.multiple_of((where[0] + away) % chips * rows, 16), rows)


class Rows:
    def __init__(self, blocks, experts, cap):
        self.blocks, self.experts = blocks, experts
        self.main = cap // 8 * 8
        self.rest = cap - self.main
        self.tile = experts * self.rest
        self.per = blocks * self.main
        self.tail = blocks * self.tile
        self.start = experts * self.per
        self.half = self.start + self.tail

    def tail_of(self, e):
        row = lax.broadcasted_iota(jnp.int32, (self.tail, 1), 0)
        return row % self.tile // self.rest == e

    def of_expert(self, ref, e):
        return jnp.concatenate([ref[e * self.per:(e + 1) * self.per, :], ref[self.start:, :]], axis=0)

    def tails(self, totals):
        out = totals[0][self.per:]
        for e in range(1, self.experts):
            out = jnp.where(self.tail_of(e), totals[e][self.per:], out)
        return out

    def regroup(self, read, out):
        for j in range(self.blocks):
            for e in range(self.experts):
                out[e * self.per + j * self.main:e * self.per + (j + 1) * self.main, :] = (
                    read(j)[e * self.main:(e + 1) * self.main, :])
        first = self.experts * self.main
        for j in range(0, self.blocks, 2):
            pair = jnp.concatenate([read(j)[first:, :], read(j + 1)[first:, :]], axis=0)
            out[self.start + j * self.tile:self.start + (j + 2) * self.tile, :] = pair

    def ungroup(self, totals, out):
        tails = self.tails(totals)
        first = self.experts * self.main
        for j in range(self.blocks):
            for e in range(self.experts):
                out[j, e * self.main:(e + 1) * self.main, :] = totals[e][j * self.main:(j + 1) * self.main]
            out[j, first:, :] = tails[j * self.tile:(j + 1) * self.tile]


def regroup_kernel(lay, where, x_ref, keep_ref, give_ref):
    for out, core in ((keep_ref, where[1]), (give_ref, 1 - where[1])):
        lay.regroup(lambda j: x_ref[core * lay.blocks + j], out)


def regroup(where, x, lay):
    vmem = pl.BlockSpec(memory_space=pltpu.VMEM)
    shape = jax.ShapeDtypeStruct((lay.half, x.shape[2]), BF16)
    return pl.pallas_call(
        functools.partial(regroup_kernel, lay),
        in_specs=[pl.BlockSpec(memory_space=pltpu.SMEM), vmem],
        out_specs=[vmem, vmem],
        out_shape=[shape, shape],
        name="regroup",
    )(where, x)


def gate_up_kernel(lay, where, x_ref, other_ref, gm, go, um, uo, up_ref, down_ref, keep_ref, own_ref, x_by, acc):
    rows = own_ref.shape[1]
    chips = lay.half // rows

    @pl.when(pl.program_id(0) == 0)
    def _():
        for e in range(lay.experts):
            x_by[e] = lay.of_expert(x_ref, e)
            x_by[lay.experts + e] = lay.of_expert(other_ref, e)

    for i, (wm, wo) in enumerate(((gm, go), (um, uo))):
        totals = []
        for e in range(lay.experts):
            total = dot(x_by[e], wm[e], 1, 0) + dot(x_by[lay.experts + e], wo[e], 1, 0)
            acc[i, e * lay.per:(e + 1) * lay.per, :] = total[:lay.per]
            totals.append(total)
        acc[i, lay.start:, :] = lay.tails(totals)
    at = functools.partial(chunk_rows, where, chips=chips, rows=rows)
    up_ref[0] = acc[0, at(2), :].astype(BF16)
    up_ref[1] = acc[1, at(1), :].astype(BF16)
    down_ref[0] = acc[1, at(2), :].astype(BF16)
    down_ref[1] = acc[0, at(chips - 1), :].astype(BF16)
    keep_ref[0] = acc[0, at(1), :]
    keep_ref[1] = acc[1, at(chips - 1), :]
    own_ref[0] = acc[0, at(0), :]
    own_ref[1] = acc[1, at(0), :]


def gate_up(where, x, other, gm, go, um, uo, lay, rows):
    experts, feats, width = gm.shape
    tile = 256
    weight = pl.BlockSpec((experts, feats, tile), lambda n, w: (0, 0, n))
    out = pl.BlockSpec((2, rows, tile), lambda n, w: (0, 0, n))
    shape = (2, rows, width)
    return pl.pallas_call(
        functools.partial(gate_up_kernel, lay),
        grid_spec=pltpu.PrefetchScalarGridSpec(
            num_scalar_prefetch=1,
            grid=(width // tile,),
            in_specs=[
                pl.BlockSpec(x.shape, lambda n, w: (0, 0)),
                pl.BlockSpec(other.shape, lambda n, w: (0, 0)),
                weight, weight, weight, weight,
            ],
            out_specs=[out, out, out, out],
            scratch_shapes=[
                pltpu.VMEM((2 * experts, lay.per + lay.tail, feats), BF16),
                pltpu.VMEM((2, lay.half, tile), F32),
            ],
        ),
        out_shape=[
            jax.ShapeDtypeStruct(shape, BF16),
            jax.ShapeDtypeStruct(shape, BF16),
            jax.ShapeDtypeStruct(shape, F32),
            jax.ShapeDtypeStruct(shape, F32),
        ],
        name="gate_up",
    )(where, x, other, gm, go, um, uo)


def hidden_grad_kernel(lay, where, g_ref, other_ref, dm, do, up_ref, down_ref, keep_ref, own_ref, g_by, acc):
    part = own_ref.shape[1]
    rows = 2 * part
    chips = lay.half // rows

    @pl.when(pl.program_id(0) == 0)
    def _():
        for e in range(lay.experts):
            g_by[e] = lay.of_expert(g_ref, e)
            g_by[lay.experts + e] = lay.of_expert(other_ref, e)

    totals = []
    for e in range(lay.experts):
        total = dot(g_by[e], dm[e], 1, 1) + dot(g_by[lay.experts + e], do[e], 1, 1)
        acc[e * lay.per:(e + 1) * lay.per, :] = total[:lay.per]
        totals.append(total)
    acc[lay.start:, :] = lay.tails(totals)

    def at(away, k):
        start = (where[0] + away) % chips * rows + k * part
        return acc[pl.ds(pl.multiple_of(start, 16), part), :]

    up_ref[0] = at(2, 0).astype(BF16)
    up_ref[1] = at(1, 1).astype(BF16)
    down_ref[0] = at(2, 1).astype(BF16)
    down_ref[1] = at(chips - 1, 0).astype(BF16)
    keep_ref[0] = at(1, 0)
    keep_ref[1] = at(chips - 1, 1)
    own_ref[0] = at(0, 0)
    own_ref[1] = at(0, 1)


def hidden_grad_parts(where, g, other, dm, do, lay, rows):
    experts, width, feats = dm.shape
    tile = 256
    weight = pl.BlockSpec((experts, tile, feats), lambda n, w: (0, n, 0))
    out = pl.BlockSpec((2, rows // 2, tile), lambda n, w: (0, 0, n))
    shape = (2, rows // 2, width)
    return pl.pallas_call(
        functools.partial(hidden_grad_kernel, lay),
        grid_spec=pltpu.PrefetchScalarGridSpec(
            num_scalar_prefetch=1,
            grid=(width // tile,),
            in_specs=[
                pl.BlockSpec(g.shape, lambda n, w: (0, 0)),
                pl.BlockSpec(other.shape, lambda n, w: (0, 0)),
                weight, weight,
            ],
            out_specs=[out, out, out, out],
            scratch_shapes=[
                pltpu.VMEM((2 * experts, lay.per + lay.tail, feats), BF16),
                pltpu.VMEM((lay.half, tile), F32),
            ],
        ),
        out_shape=[
            jax.ShapeDtypeStruct(shape, BF16),
            jax.ShapeDtypeStruct(shape, BF16),
            jax.ShapeDtypeStruct(shape, F32),
            jax.ShapeDtypeStruct(shape, F32),
        ],
        name="hidden_grad",
    )(where, g, other, dm, do)


def gather_rows(where, put_to, own, low, high, far, chips, rows):
    def put(away, value, skip=0):
        start = (where[0] + away) % chips * rows + skip
        put_to(pl.ds(pl.multiple_of(start, 16), value.shape[0]), value)

    put(0, own)
    put(chips - 1, low)
    put(1, high)
    skip = 0
    for value in far:
        put(2, value, skip)
        skip += value.shape[0]


def expert_out_kernel(lay, where, own, low, high, far_a, far_b, dm, do, mine_ref, other_ref, all_ref):
    rows = own.shape[0]

    def put_to(at, value):
        all_ref[at, :] = value

    gather_rows(where, put_to, own[...], low[...], high[...], (far_a[...], far_b[...]), lay.half // rows, rows)
    for out, weight in ((mine_ref, dm), (other_ref, do)):
        totals = [dot(lay.of_expert(all_ref, e), weight[e], 1, 0).astype(BF16) for e in range(lay.experts)]
        lay.ungroup(totals, out)


def expert_out_of(where, pieces, dm, do, lay):
    experts, width, feats = dm.shape
    vmem = pl.BlockSpec(memory_space=pltpu.VMEM)
    out = jax.ShapeDtypeStruct((lay.blocks, experts * lay.main + lay.tile, feats), BF16)
    return pl.pallas_call(
        functools.partial(expert_out_kernel, lay),
        in_specs=[pl.BlockSpec(memory_space=pltpu.SMEM)] + [vmem] * 7,
        out_specs=[vmem] * 3,
        out_shape=[out, out, jax.ShapeDtypeStruct((lay.half, width), BF16)],
        name="expert_out",
    )(where, *pieces, dm, do)


def slot_in_kernel(lay, where, own, low, high, far_g, far_u, gm, go, um, uo, mine_ref, other_ref, all_ref):
    rows = own.shape[1]
    for i, far in enumerate((far_g, far_u)):

        def put_to(at, value):
            all_ref[i, at, :] = value

        gather_rows(where, put_to, own[i], low[i], high[i], (far[...],), lay.half // rows, rows)
    for out, gw, uw in ((mine_ref, gm, um), (other_ref, go, uo)):
        totals = []
        for e in range(lay.experts):
            total = dot(lay.of_expert(all_ref.at[0], e), gw[e], 1, 1)
            totals.append((total + dot(lay.of_expert(all_ref.at[1], e), uw[e], 1, 1)).astype(BF16))
        lay.ungroup(totals, out)


def slot_in_of(where, pieces, gm, go, um, uo, lay):
    experts, feats, width = gm.shape
    vmem = pl.BlockSpec(memory_space=pltpu.VMEM)
    out = jax.ShapeDtypeStruct((lay.blocks, experts * lay.main + lay.tile, feats), BF16)
    return pl.pallas_call(
        functools.partial(slot_in_kernel, lay),
        in_specs=[pl.BlockSpec(memory_space=pltpu.SMEM)] + [vmem] * 9,
        out_specs=[vmem] * 3,
        out_shape=[out, out, jax.ShapeDtypeStruct((2, lay.half, width), BF16)],
        name="slot_in",
    )(where, *pieces, gm, go, um, uo)


def routing(ids, weight, owner, rank, allowed, block, experts_all):
    rows = ids.shape[0]
    experts = jnp.arange(experts_all, dtype=jnp.int32)
    hit = ids[:, :, None] == experts[None, None, :]
    member = jnp.any(hit, axis=1)
    t_row = lax.broadcasted_iota(jnp.int32, (rows, rows), 0)
    t_col = lax.broadcasted_iota(jnp.int32, (rows, rows), 1)
    earlier = ((t_col <= t_row) & (t_col // block == t_row // block)).astype(BF16)
    rank1 = jnp.where(member, dot(earlier, member.astype(BF16), 1, 0), 0.0)
    spread = (experts[:, None] == owner[None, :]).astype(BF16)
    rank1_s = dot(rank1.astype(BF16), spread, 1, 0)
    taken = rank1_s == (rank + 1).astype(F32)[None, :]
    if allowed is not None:
        taken = taken & allowed
    if weight is None:
        return taken.astype(BF16)
    weight_te = jnp.sum(jnp.where(hit, weight[:, :, None], 0.0), axis=1)
    weight_s = sum(dot(part, spread, 1, 0) for part in split3(weight_te))
    return taken.astype(BF16), jnp.where(taken, weight_s, 0.0)


def weighted_sum(weight_s, rows):
    return sum(dot(part, rows, 1, 0) for part in split3(weight_s))


def layer(tokens, out_grad, expert_ids, route_weight, gate_weight, up_weight, down_weight):
    n_y, n_z, n_x = (lax.axis_size(a) for a in ("y", "z_lo", "x"))
    n_cols = n_y * n_z * n_x
    n_reps = lax.axis_size("replica")
    tok_count, topk = expert_ids.shape
    local_experts, feats, _ = gate_weight.shape
    experts_all = local_experts * n_cols
    cap = tok_count * topk * 5 // (4 * experts_all)
    slots = experts_all * cap
    rows = slots // n_reps

    rep = lax.axis_index("replica")
    core = rep % CORES
    where = jnp.stack([rep // CORES, core]).astype(jnp.int32)
    to_swap = [(r, r ^ 1) for r in range(n_reps)]
    to_up = [(r, (r + CORES) % n_reps) for r in range(n_reps)]
    to_down = [(r, (r - CORES) % n_reps) for r in range(n_reps)]

    def swap(a):
        return lax.ppermute(a, "replica", to_swap)

    def up_one(a):
        return lax.ppermute(a, "replica", to_up)

    def down_one(a):
        return lax.ppermute(a, "replica", to_down)

    def tree_sum(send_up, send_down, keep, own):
        low = up_one(send_up)
        high = down_one(send_down)
        first = up_one((keep[0] + low[0].astype(F32)).astype(BF16))
        second = down_one((keep[1] + high[0].astype(F32)).astype(BF16))
        a = own[0] + high[1].astype(F32) + first.astype(F32)
        b = own[1] + low[1].astype(F32) + second.astype(F32)
        return a, b

    plane = n_y * n_x
    z_lo = lax.axis_index("z_lo")
    to_plane = [(z, n_z - 1 - z) for z in range(n_z)]
    lay = Rows(n_cols // CORES, local_experts, cap)

    def cross(a):
        return lax.ppermute(a, "z_lo", to_plane)

    def by_plane(mine, far):
        first = lax.select_n(z_lo == 0, far, mine)
        return jnp.concatenate([first, lax.select_n(z_lo == 0, mine, far)], axis=0)

    gate_other = swap(gate_weight)
    up_other = swap(up_weight)
    down_other = swap(down_weight)
    pairs = jnp.concatenate([expert_ids.astype(F32), route_weight], axis=1)
    pairs_other = cross(pairs)
    out_grad_other = cross(out_grad)

    block_rows = local_experts * cap
    slot = jnp.arange(slots, dtype=jnp.int32)
    at, inner = slot // block_rows, slot % block_rows
    first = local_experts * lay.main
    which = jnp.where(inner < first, inner // lay.main, (inner - first) // lay.rest)
    rank = jnp.where(inner < first, inner % lay.main, lay.main + (inner - first) % lay.rest)

    def owner_of(z):
        return (((at // n_z // n_x) * n_z + z) * n_x + at // n_z % n_x) * local_experts + which

    picker = routing(expert_ids, None, owner_of(at % n_z), rank, None, tok_count, experts_all)
    send_x = dot(picker, tokens, 0, 0).astype(BF16)

    def exchange(a):
        a = a.reshape(n_cols, block_rows, feats)
        return lax.all_to_all(a, ("y", "x", "z_lo"), split_axis=0, concat_axis=0, tiled=True)

    def exchange_plane(a):
        a = a.reshape(plane, n_z * block_rows, feats)
        return lax.all_to_all(a, ("y", "x"), split_axis=0, concat_axis=0, tiled=True)

    def both_halves(mine, other):
        got = swap(other)
        return jnp.concatenate(
            [lax.select_n(core == 0, got, mine), lax.select_n(core == 0, mine, got)], axis=0)

    recv_x = exchange(send_x)
    x_keep, x_give = regroup(where, recv_x, lay)
    x_other = swap(x_give)

    token = jnp.arange(n_z * tok_count, dtype=jnp.int32)
    same = token[:, None] // tok_count == at[None, :] % n_z
    pairs2 = by_plane(pairs, pairs_other)
    picker2, weight2 = routing(
        pairs2[:, :topk].astype(jnp.int32), pairs2[:, topk:],
        owner_of(z_lo), rank, same, tok_count, experts_all)
    picked_g = dot(picker2, by_plane(out_grad, out_grad_other), 0, 0)
    send_g = (jnp.sum(weight2, axis=0)[:, None] * picked_g).astype(BF16)
    recv_g = exchange_plane(send_g).reshape(n_cols, block_rows, feats)

    gate, up = tree_sum(*gate_up(
        where, x_keep, x_other, gate_weight, gate_other, up_weight, up_other, lay, rows))

    g_keep, g_give = regroup(where, recv_g, lay)
    g_other = swap(g_give)
    grad_a, grad_b = tree_sum(*hidden_grad_parts(where, g_keep, g_other, down_weight, down_other, lay, rows))
    hidden_grad = jnp.concatenate([grad_a, grad_b], axis=0)

    own = (gate * jax.nn.sigmoid(gate) * up).astype(BF16)
    low, high = up_one(own), down_one(own)
    far_a, far_b = up_one(low[:rows // 2]), down_one(high[rows // 2:])
    mine, other, hidden = expert_out_of(
        where, (own, low, high, far_a, far_b), down_weight, down_other, lay)
    expert_out = both_halves(mine, other)
    returned = exchange_plane(expert_out).reshape(slots, feats)
    sums = weighted_sum(weight2, returned).reshape(n_z, tok_count, feats)
    mine = lax.select_n(z_lo == 0, sums[1], sums[0])
    from_far = cross(lax.select_n(z_lo == 0, sums[0], sums[1]))
    mixed = (mine + from_far).astype(BF16)

    gate, up = lax.optimization_barrier((gate, up))
    sig = jax.nn.sigmoid(gate)
    gate_grad = (hidden_grad * up * sig * (1.0 + gate * (1.0 - sig))).astype(BF16)
    up_grad = (hidden_grad * (gate * sig)).astype(BF16)
    own = jnp.stack([gate_grad, up_grad])
    low, high = up_one(own), down_one(own)
    far_g, far_u = up_one(low[0]), down_one(high[1])
    mine, other, grads = slot_in_of(
        where, (own, low, high, far_g, far_u), gate_weight, gate_other, up_weight, up_other, lay)
    slot_in = both_halves(mine, other)
    back_in = exchange(slot_in).reshape(slots, feats)
    in_grad = dot(picker, back_in, 1, 0).astype(BF16)

    row = jnp.arange(lay.half, dtype=jnp.int32)[:, None]
    expert_of = jnp.where(row < lay.start, row // lay.per, (row - lay.start) % lay.tile // lay.rest)

    def by_expert(a):
        masked = [jnp.where(expert_of == e, a, jnp.zeros((), a.dtype)) for e in range(local_experts)]
        return jnp.concatenate(masked, axis=1)

    def over_halves(a, b, c, d):
        return (dot(a, c, 0, 0) + dot(b, d, 0, 0)).astype(BF16)

    hidden_other = swap(hidden)
    grad_down = over_halves(by_expert(hidden), by_expert(hidden_other), g_keep, g_give)
    grads_other = swap(grads)
    x_own, x_far = by_expert(x_keep), by_expert(x_give)
    grad_gate = over_halves(x_own, x_far, grads[0], grads_other[0])
    grad_up = over_halves(x_own, x_far, grads[1], grads_other[1])
    return (
        mixed,
        in_grad,
        grad_gate.reshape(gate_weight.shape),
        grad_up.reshape(up_weight.shape),
        grad_down.reshape(down_weight.shape),
    )


def solution(mesh):
    n_y, n_z, n_x = 4, 2, 4
    devices = mesh.devices.reshape(n_y, n_z, n_x, mesh.shape["replica"])
    mesh = Mesh(devices, ("y", "z_lo", "x", "replica"))
    cols = ("y", "z_lo", "x")
    in_specs = (
        P(cols, "replica"),
        P(cols, "replica"),
        P(cols, None),
        P(cols, None),
        P(cols, "replica", None),
        P(cols, "replica", None),
        P(cols, None, "replica"),
    )
    out_specs = (
        P(cols, "replica"),
        P(cols, "replica"),
        P(cols, "replica", None),
        P(cols, "replica", None),
        P(cols, None, "replica"),
    )
    return jax.shard_map(layer, mesh=mesh, in_specs=in_specs, out_specs=out_specs, check_vma=False)
```

```python
import functools
import jax
import jax.numpy as jnp
from jax import lax
from jax.experimental import pallas as pl
from jax.experimental.pallas import tpu as pltpu
from jax.sharding import Mesh, PartitionSpec as P


F32 = jnp.float32
BF16 = jnp.bfloat16
CORES = 2


def dot(a, b, ca, cb):
    return lax.dot_general(a, b, (((ca,), (cb,)), ((), ())), preferred_element_type=F32)


def split3(w):
    hi = w.astype(BF16)
    rest = w - hi.astype(F32)
    mid = rest.astype(BF16)
    low = (rest - mid.astype(F32)).astype(BF16)
    return hi, mid, low


def chunk_rows(where, away, chips, rows):
    return pl.ds(pl.multiple_of((where[0] + away) % chips * rows, 16), rows)


class Rows:
    def __init__(self, blocks, experts, cap):
        self.blocks, self.experts = blocks, experts
        self.main = cap // 8 * 8
        self.rest = cap - self.main
        self.tile = experts * self.rest
        self.per = blocks * self.main
        self.tail = blocks * self.tile
        self.start = experts * self.per
        self.half = self.start + self.tail

    def tail_of(self, e):
        row = lax.broadcasted_iota(jnp.int32, (self.tail, 1), 0)
        return row % self.tile // self.rest == e

    def of_expert(self, ref, e):
        return jnp.concatenate([ref[e * self.per:(e + 1) * self.per, :], ref[self.start:, :]], axis=0)

    def tails(self, totals):
        out = totals[0][self.per:]
        for e in range(1, self.experts):
            out = jnp.where(self.tail_of(e), totals[e][self.per:], out)
        return out

    def regroup(self, read, out):
        for j in range(self.blocks):
            for e in range(self.experts):
                out[e * self.per + j * self.main:e * self.per + (j + 1) * self.main, :] = (
                    read(j)[e * self.main:(e + 1) * self.main, :])
        first = self.experts * self.main
        for j in range(0, self.blocks, 2):
            pair = jnp.concatenate([read(j)[first:, :], read(j + 1)[first:, :]], axis=0)
            out[self.start + j * self.tile:self.start + (j + 2) * self.tile, :] = pair

    def ungroup(self, totals, out):
        tails = self.tails(totals)
        first = self.experts * self.main
        for j in range(self.blocks):
            for e in range(self.experts):
                out[j, e * self.main:(e + 1) * self.main, :] = totals[e][j * self.main:(j + 1) * self.main]
            out[j, first:, :] = tails[j * self.tile:(j + 1) * self.tile]


def regroup_kernel(lay, where, x_ref, keep_ref, give_ref):
    for out, core in ((keep_ref, where[1]), (give_ref, 1 - where[1])):
        lay.regroup(lambda j: x_ref[core * lay.blocks + j], out)


def regroup(where, x, lay):
    vmem = pl.BlockSpec(memory_space=pltpu.VMEM)
    shape = jax.ShapeDtypeStruct((lay.half, x.shape[2]), BF16)
    return pl.pallas_call(
        functools.partial(regroup_kernel, lay),
        in_specs=[pl.BlockSpec(memory_space=pltpu.SMEM), vmem],
        out_specs=[vmem, vmem],
        out_shape=[shape, shape],
        name="regroup",
    )(where, x)


def gate_up_kernel(lay, where, x_ref, other_ref, gm, go, um, uo, up_ref, down_ref, keep_ref, own_ref, x_by, acc):
    rows = own_ref.shape[1]
    chips = lay.half // rows

    @pl.when(pl.program_id(0) == 0)
    def _():
        for e in range(lay.experts):
            x_by[e] = lay.of_expert(x_ref, e)
            x_by[lay.experts + e] = lay.of_expert(other_ref, e)

    for i, (wm, wo) in enumerate(((gm, go), (um, uo))):
        totals = []
        for e in range(lay.experts):
            total = dot(x_by[e], wm[e], 1, 0) + dot(x_by[lay.experts + e], wo[e], 1, 0)
            acc[i, e * lay.per:(e + 1) * lay.per, :] = total[:lay.per]
            totals.append(total)
        acc[i, lay.start:, :] = lay.tails(totals)
    at = functools.partial(chunk_rows, where, chips=chips, rows=rows)
    up_ref[0] = acc[0, at(2), :].astype(BF16)
    up_ref[1] = acc[1, at(1), :].astype(BF16)
    down_ref[0] = acc[1, at(2), :].astype(BF16)
    down_ref[1] = acc[0, at(chips - 1), :].astype(BF16)
    keep_ref[0] = acc[0, at(1), :]
    keep_ref[1] = acc[1, at(chips - 1), :]
    own_ref[0] = acc[0, at(0), :]
    own_ref[1] = acc[1, at(0), :]


def gate_up(where, x, other, gm, go, um, uo, lay, rows):
    experts, feats, width = gm.shape
    tile = 256
    weight = pl.BlockSpec((experts, feats, tile), lambda n, w: (0, 0, n))
    out = pl.BlockSpec((2, rows, tile), lambda n, w: (0, 0, n))
    shape = (2, rows, width)
    return pl.pallas_call(
        functools.partial(gate_up_kernel, lay),
        grid_spec=pltpu.PrefetchScalarGridSpec(
            num_scalar_prefetch=1,
            grid=(width // tile,),
            in_specs=[
                pl.BlockSpec(x.shape, lambda n, w: (0, 0)),
                pl.BlockSpec(other.shape, lambda n, w: (0, 0)),
                weight, weight, weight, weight,
            ],
            out_specs=[out, out, out, out],
            scratch_shapes=[
                pltpu.VMEM((2 * experts, lay.per + lay.tail, feats), BF16),
                pltpu.VMEM((2, lay.half, tile), F32),
            ],
        ),
        out_shape=[
            jax.ShapeDtypeStruct(shape, BF16),
            jax.ShapeDtypeStruct(shape, BF16),
            jax.ShapeDtypeStruct(shape, F32),
            jax.ShapeDtypeStruct(shape, F32),
        ],
        name="gate_up",
    )(where, x, other, gm, go, um, uo)


def hidden_grad_kernel(lay, where, g_ref, other_ref, dm, do, up_ref, down_ref, keep_ref, own_ref, g_by, acc):
    part = own_ref.shape[1]
    rows = 2 * part
    chips = lay.half // rows

    @pl.when(pl.program_id(0) == 0)
    def _():
        for e in range(lay.experts):
            g_by[e] = lay.of_expert(g_ref, e)
            g_by[lay.experts + e] = lay.of_expert(other_ref, e)

    totals = []
    for e in range(lay.experts):
        total = dot(g_by[e], dm[e], 1, 1) + dot(g_by[lay.experts + e], do[e], 1, 1)
        acc[e * lay.per:(e + 1) * lay.per, :] = total[:lay.per]
        totals.append(total)
    acc[lay.start:, :] = lay.tails(totals)

    def at(away, k):
        start = (where[0] + away) % chips * rows + k * part
        return acc[pl.ds(pl.multiple_of(start, 16), part), :]

    up_ref[0] = at(2, 0).astype(BF16)
    up_ref[1] = at(1, 1).astype(BF16)
    down_ref[0] = at(2, 1).astype(BF16)
    down_ref[1] = at(chips - 1, 0).astype(BF16)
    keep_ref[0] = at(1, 0)
    keep_ref[1] = at(chips - 1, 1)
    own_ref[0] = at(0, 0)
    own_ref[1] = at(0, 1)


def hidden_grad_parts(where, g, other, dm, do, lay, rows):
    experts, width, feats = dm.shape
    tile = 256
    weight = pl.BlockSpec((experts, tile, feats), lambda n, w: (0, n, 0))
    out = pl.BlockSpec((2, rows // 2, tile), lambda n, w: (0, 0, n))
    shape = (2, rows // 2, width)
    return pl.pallas_call(
        functools.partial(hidden_grad_kernel, lay),
        grid_spec=pltpu.PrefetchScalarGridSpec(
            num_scalar_prefetch=1,
            grid=(width // tile,),
            in_specs=[
                pl.BlockSpec(g.shape, lambda n, w: (0, 0)),
                pl.BlockSpec(other.shape, lambda n, w: (0, 0)),
                weight, weight,
            ],
            out_specs=[out, out, out, out],
            scratch_shapes=[
                pltpu.VMEM((2 * experts, lay.per + lay.tail, feats), BF16),
                pltpu.VMEM((lay.half, tile), F32),
            ],
        ),
        out_shape=[
            jax.ShapeDtypeStruct(shape, BF16),
            jax.ShapeDtypeStruct(shape, BF16),
            jax.ShapeDtypeStruct(shape, F32),
            jax.ShapeDtypeStruct(shape, F32),
        ],
        name="hidden_grad",
    )(where, g, other, dm, do)


def gather_rows(where, put_to, own, low, high, far, chips, rows):
    def put(away, value, skip=0):
        start = (where[0] + away) % chips * rows + skip
        put_to(pl.ds(pl.multiple_of(start, 16), value.shape[0]), value)

    put(0, own)
    put(chips - 1, low)
    put(1, high)
    skip = 0
    for value in far:
        put(2, value, skip)
        skip += value.shape[0]


def expert_out_kernel(lay, where, own, low, high, far_a, far_b, dm, do, mine_ref, other_ref, all_ref):
    rows = own.shape[0]

    def put_to(at, value):
        all_ref[at, :] = value

    gather_rows(where, put_to, own[...], low[...], high[...], (far_a[...], far_b[...]), lay.half // rows, rows)
    for out, weight in ((mine_ref, dm), (other_ref, do)):
        totals = [dot(lay.of_expert(all_ref, e), weight[e], 1, 0).astype(BF16) for e in range(lay.experts)]
        lay.ungroup(totals, out)


def expert_out_of(where, pieces, dm, do, lay):
    experts, width, feats = dm.shape
    vmem = pl.BlockSpec(memory_space=pltpu.VMEM)
    out = jax.ShapeDtypeStruct((lay.blocks, experts * lay.main + lay.tile, feats), BF16)
    return pl.pallas_call(
        functools.partial(expert_out_kernel, lay),
        in_specs=[pl.BlockSpec(memory_space=pltpu.SMEM)] + [vmem] * 7,
        out_specs=[vmem] * 3,
        out_shape=[out, out, jax.ShapeDtypeStruct((lay.half, width), BF16)],
        name="expert_out",
    )(where, *pieces, dm, do)


def slot_in_kernel(lay, where, own, low, high, far_g, far_u, gm, go, um, uo, mine_ref, other_ref, all_ref):
    rows = own.shape[1]
    for i, far in enumerate((far_g, far_u)):

        def put_to(at, value):
            all_ref[i, at, :] = value

        gather_rows(where, put_to, own[i], low[i], high[i], (far[...],), lay.half // rows, rows)
    for out, gw, uw in ((mine_ref, gm, um), (other_ref, go, uo)):
        totals = []
        for e in range(lay.experts):
            total = dot(lay.of_expert(all_ref.at[0], e), gw[e], 1, 1)
            totals.append((total + dot(lay.of_expert(all_ref.at[1], e), uw[e], 1, 1)).astype(BF16))
        lay.ungroup(totals, out)


def slot_in_of(where, pieces, gm, go, um, uo, lay):
    experts, feats, width = gm.shape
    vmem = pl.BlockSpec(memory_space=pltpu.VMEM)
    out = jax.ShapeDtypeStruct((lay.blocks, experts * lay.main + lay.tile, feats), BF16)
    return pl.pallas_call(
        functools.partial(slot_in_kernel, lay),
        in_specs=[pl.BlockSpec(memory_space=pltpu.SMEM)] + [vmem] * 9,
        out_specs=[vmem] * 3,
        out_shape=[out, out, jax.ShapeDtypeStruct((2, lay.half, width), BF16)],
        name="slot_in",
    )(where, *pieces, gm, go, um, uo)


def weight_grad_kernel(lay, a_own, a_far, b_own, b_far, out_ref, a_by, b_by):
    e = pl.program_id(0)
    main = pl.ds(pl.multiple_of(e * lay.per, 16), lay.per)
    at = [pl.ds(0, lay.per), pl.ds(lay.per, lay.per)]
    rest = [pl.ds(2 * lay.per, lay.tail), pl.ds(2 * lay.per + lay.tail, lay.tail)]

    @pl.when(pl.program_id(1) == 0)
    def _():
        for k, ref in enumerate((a_own, a_far)):
            a_by[at[k], :] = ref[main, :]
            tail = ref[lay.start:, :]
            a_by[rest[k], :] = jnp.where(lay.tail_of(e), tail, jnp.zeros_like(tail))

    for k, ref in enumerate((b_own, b_far)):
        b_by[at[k], :] = ref[0, main, :]
        b_by[rest[k], :] = ref[0, lay.start:, :]
    out_ref[0] = dot(a_by[...], b_by[...], 0, 0).astype(BF16)


def weight_grad(a_own, a_far, b_own, b_far, i, lay):
    rows = 2 * (lay.per + lay.tail)
    a_cols, b_cols = a_own.shape[1], b_own.shape[2]
    tile = 256
    a_spec = pl.BlockSpec(a_own.shape, lambda e, n: (0, 0))
    b_spec = pl.BlockSpec((1, lay.half, tile), lambda e, n: (i, 0, n))
    return pl.pallas_call(
        functools.partial(weight_grad_kernel, lay),
        grid=(lay.experts, b_cols // tile),
        in_specs=[a_spec, a_spec, b_spec, b_spec],
        out_specs=pl.BlockSpec((1, a_cols, tile), lambda e, n: (e, 0, n)),
        out_shape=jax.ShapeDtypeStruct((lay.experts, a_cols, b_cols), BF16),
        scratch_shapes=[pltpu.VMEM((rows, a_cols), BF16), pltpu.VMEM((rows, tile), BF16)],
        name="weight_grad",
    )(a_own, a_far, b_own, b_far)


def routing(ids, weight, owner, rank, allowed, block, experts_all):
    rows = ids.shape[0]
    experts = jnp.arange(experts_all, dtype=jnp.int32)
    hit = ids[:, :, None] == experts[None, None, :]
    member = jnp.any(hit, axis=1)
    t_row = lax.broadcasted_iota(jnp.int32, (rows, rows), 0)
    t_col = lax.broadcasted_iota(jnp.int32, (rows, rows), 1)
    earlier = ((t_col <= t_row) & (t_col // block == t_row // block)).astype(BF16)
    rank1 = jnp.where(member, dot(earlier, member.astype(BF16), 1, 0), 0.0)
    spread = (experts[:, None] == owner[None, :]).astype(BF16)
    rank1_s = dot(rank1.astype(BF16), spread, 1, 0)
    taken = rank1_s == (rank + 1).astype(F32)[None, :]
    if allowed is not None:
        taken = taken & allowed
    if weight is None:
        return taken.astype(BF16)
    weight_te = jnp.sum(jnp.where(hit, weight[:, :, None], 0.0), axis=1)
    weight_s = sum(dot(part, spread, 1, 0) for part in split3(weight_te))
    return taken.astype(BF16), jnp.where(taken, weight_s, 0.0)


def weighted_sum(weight_s, rows):
    return sum(dot(part, rows, 1, 0) for part in split3(weight_s))


def layer(tokens, out_grad, expert_ids, route_weight, gate_weight, up_weight, down_weight):
    n_y, n_z, n_x = (lax.axis_size(a) for a in ("y", "z_lo", "x"))
    n_cols = n_y * n_z * n_x
    n_reps = lax.axis_size("replica")
    tok_count, topk = expert_ids.shape
    local_experts, feats, _ = gate_weight.shape
    experts_all = local_experts * n_cols
    cap = tok_count * topk * 5 // (4 * experts_all)
    slots = experts_all * cap
    rows = slots // n_reps

    rep = lax.axis_index("replica")
    core = rep % CORES
    where = jnp.stack([rep // CORES, core]).astype(jnp.int32)
    to_swap = [(r, r ^ 1) for r in range(n_reps)]
    to_up = [(r, (r + CORES) % n_reps) for r in range(n_reps)]
    to_down = [(r, (r - CORES) % n_reps) for r in range(n_reps)]

    def swap(a):
        return lax.ppermute(a, "replica", to_swap)

    def up_one(a):
        return lax.ppermute(a, "replica", to_up)

    def down_one(a):
        return lax.ppermute(a, "replica", to_down)

    def tree_sum(send_up, send_down, keep, own):
        low = up_one(send_up)
        high = down_one(send_down)
        first = up_one((keep[0] + low[0].astype(F32)).astype(BF16))
        second = down_one((keep[1] + high[0].astype(F32)).astype(BF16))
        a = own[0] + high[1].astype(F32) + first.astype(F32)
        b = own[1] + low[1].astype(F32) + second.astype(F32)
        return a, b

    plane = n_y * n_x
    z_lo = lax.axis_index("z_lo")
    to_plane = [(z, n_z - 1 - z) for z in range(n_z)]
    lay = Rows(n_cols // CORES, local_experts, cap)

    def cross(a):
        return lax.ppermute(a, "z_lo", to_plane)

    def by_plane(mine, far):
        first = lax.select_n(z_lo == 0, far, mine)
        return jnp.concatenate([first, lax.select_n(z_lo == 0, mine, far)], axis=0)

    gate_other = swap(gate_weight)
    up_other = swap(up_weight)
    down_other = swap(down_weight)
    pairs = jnp.concatenate([expert_ids.astype(F32), route_weight], axis=1)
    pairs_other = cross(pairs)
    out_grad_other = cross(out_grad)

    block_rows = local_experts * cap
    slot = jnp.arange(slots, dtype=jnp.int32)
    at, inner = slot // block_rows, slot % block_rows
    first = local_experts * lay.main
    which = jnp.where(inner < first, inner // lay.main, (inner - first) // lay.rest)
    rank = jnp.where(inner < first, inner % lay.main, lay.main + (inner - first) % lay.rest)

    def owner_of(z):
        return (((at // n_z // n_x) * n_z + z) * n_x + at // n_z % n_x) * local_experts + which

    picker = routing(expert_ids, None, owner_of(at % n_z), rank, None, tok_count, experts_all)
    send_x = dot(picker, tokens, 0, 0).astype(BF16)

    def exchange(a):
        a = a.reshape(n_cols, block_rows, feats)
        return lax.all_to_all(a, ("y", "x", "z_lo"), split_axis=0, concat_axis=0, tiled=True)

    def exchange_plane(a):
        a = a.reshape(plane, n_z * block_rows, feats)
        return lax.all_to_all(a, ("y", "x"), split_axis=0, concat_axis=0, tiled=True)

    def both_halves(mine, other):
        got = swap(other)
        return jnp.concatenate(
            [lax.select_n(core == 0, got, mine), lax.select_n(core == 0, mine, got)], axis=0)

    recv_x = exchange(send_x)
    x_keep, x_give = regroup(where, recv_x, lay)
    x_other = swap(x_give)

    token = jnp.arange(n_z * tok_count, dtype=jnp.int32)
    same = token[:, None] // tok_count == at[None, :] % n_z
    pairs2 = by_plane(pairs, pairs_other)
    picker2, weight2 = routing(
        pairs2[:, :topk].astype(jnp.int32), pairs2[:, topk:],
        owner_of(z_lo), rank, same, tok_count, experts_all)
    picked_g = dot(picker2, by_plane(out_grad, out_grad_other), 0, 0)
    send_g = (jnp.sum(weight2, axis=0)[:, None] * picked_g).astype(BF16)
    recv_g = exchange_plane(send_g).reshape(n_cols, block_rows, feats)

    gate, up = tree_sum(*gate_up(
        where, x_keep, x_other, gate_weight, gate_other, up_weight, up_other, lay, rows))

    g_keep, g_give = regroup(where, recv_g, lay)
    g_other = swap(g_give)
    grad_a, grad_b = tree_sum(*hidden_grad_parts(where, g_keep, g_other, down_weight, down_other, lay, rows))
    hidden_grad = jnp.concatenate([grad_a, grad_b], axis=0)

    own = (gate * jax.nn.sigmoid(gate) * up).astype(BF16)
    low, high = up_one(own), down_one(own)
    far_a, far_b = up_one(low[:rows // 2]), down_one(high[rows // 2:])
    mine, other, hidden = expert_out_of(
        where, (own, low, high, far_a, far_b), down_weight, down_other, lay)
    expert_out = both_halves(mine, other)
    returned = exchange_plane(expert_out).reshape(slots, feats)
    sums = weighted_sum(weight2, returned).reshape(n_z, tok_count, feats)
    sum_mine = lax.select_n(z_lo == 0, sums[1], sums[0])
    from_far = cross(lax.select_n(z_lo == 0, sums[0], sums[1]))

    gate, up = lax.optimization_barrier((gate, up))
    sig = jax.nn.sigmoid(gate)
    gate_grad = (hidden_grad * up * sig * (1.0 + gate * (1.0 - sig))).astype(BF16)
    up_grad = (hidden_grad * (gate * sig)).astype(BF16)
    own = jnp.stack([gate_grad, up_grad])
    low, high = up_one(own), down_one(own)
    far_g, far_u = up_one(low[0]), down_one(high[1])
    mine, other, grads = slot_in_of(
        where, (own, low, high, far_g, far_u), gate_weight, gate_other, up_weight, up_other, lay)
    slot_in = both_halves(mine, other)
    back_in = exchange(slot_in).reshape(slots, feats)
    in_grad = dot(picker, back_in, 1, 0).astype(BF16)

    hidden_other = swap(hidden)
    grad_down = weight_grad(hidden, hidden_other, g_keep[None], g_give[None], 0, lay)
    grads_other = swap(grads)
    grad_gate = weight_grad(x_keep, x_give, grads, grads_other, 0, lay)
    grad_up = weight_grad(x_keep, x_give, grads, grads_other, 1, lay)
    grad_up, sum_mine = lax.optimization_barrier((grad_up, sum_mine))
    mixed = (sum_mine + from_far).astype(BF16)
    return (mixed, in_grad, grad_gate, grad_up, grad_down)


def solution(mesh):
    n_y, n_z, n_x = 4, 2, 4
    devices = mesh.devices.reshape(n_y, n_z, n_x, mesh.shape["replica"])
    mesh = Mesh(devices, ("y", "z_lo", "x", "replica"))
    cols = ("y", "z_lo", "x")
    in_specs = (
        P(cols, "replica"),
        P(cols, "replica"),
        P(cols, None),
        P(cols, None),
        P(cols, "replica", None),
        P(cols, "replica", None),
        P(cols, None, "replica"),
    )
    out_specs = (
        P(cols, "replica"),
        P(cols, "replica"),
        P(cols, "replica", None),
        P(cols, "replica", None),
        P(cols, None, "replica"),
    )
    return jax.shard_map(layer, mesh=mesh, in_specs=in_specs, out_specs=out_specs, check_vma=False)
```

```python
import functools
import jax
import jax.numpy as jnp
from jax import lax
from jax.experimental import pallas as pl
from jax.experimental.pallas import tpu as pltpu
from jax.sharding import Mesh, PartitionSpec as P


F32 = jnp.float32
BF16 = jnp.bfloat16
CORES = 2


def dot(a, b, ca, cb):
    return lax.dot_general(a, b, (((ca,), (cb,)), ((), ())), preferred_element_type=F32)


def split3(w):
    hi = w.astype(BF16)
    rest = w - hi.astype(F32)
    mid = rest.astype(BF16)
    low = (rest - mid.astype(F32)).astype(BF16)
    return hi, mid, low


def chunk_rows(where, away, chips, rows):
    return pl.ds(pl.multiple_of((where[0] + away) % chips * rows, 16), rows)


class Rows:
    def __init__(self, blocks, experts, cap):
        self.blocks, self.experts = blocks, experts
        self.main = cap // 8 * 8
        self.rest = cap - self.main
        self.tile = experts * self.rest
        self.per = blocks * self.main
        self.tail = blocks * self.tile
        self.start = experts * self.per
        self.half = self.start + self.tail

    def tail_of(self, e):
        row = lax.broadcasted_iota(jnp.int32, (self.tail, 1), 0)
        return row % self.tile // self.rest == e

    def of_expert(self, ref, e):
        return jnp.concatenate([ref[e * self.per:(e + 1) * self.per, :], ref[self.start:, :]], axis=0)

    def tails(self, totals):
        out = totals[0][self.per:]
        for e in range(1, self.experts):
            out = jnp.where(self.tail_of(e), totals[e][self.per:], out)
        return out

    def regroup(self, read, out):
        for j in range(self.blocks):
            for e in range(self.experts):
                out[e * self.per + j * self.main:e * self.per + (j + 1) * self.main, :] = (
                    read(j)[e * self.main:(e + 1) * self.main, :])
        first = self.experts * self.main
        for j in range(0, self.blocks, 2):
            pair = jnp.concatenate([read(j)[first:, :], read(j + 1)[first:, :]], axis=0)
            out[self.start + j * self.tile:self.start + (j + 2) * self.tile, :] = pair

    def ungroup(self, totals, out, base):
        tails = self.tails(totals)
        first = self.experts * self.main
        for j in range(self.blocks):
            for e in range(self.experts):
                out[base + j, e * self.main:(e + 1) * self.main, :] = totals[e][j * self.main:(j + 1) * self.main]
            out[base + j, first:, :] = tails[j * self.tile:(j + 1) * self.tile]


def regroup_kernel(lay, where, x_ref, keep_ref, give_ref):
    for out, core in ((keep_ref, where[1]), (give_ref, 1 - where[1])):
        lay.regroup(lambda j: x_ref[core * lay.blocks + j], out)


def regroup(where, x, lay):
    vmem = pl.BlockSpec(memory_space=pltpu.VMEM)
    shape = jax.ShapeDtypeStruct((lay.half, x.shape[2]), BF16)
    return pl.pallas_call(
        functools.partial(regroup_kernel, lay),
        in_specs=[pl.BlockSpec(memory_space=pltpu.SMEM), vmem],
        out_specs=[vmem, vmem],
        out_shape=[shape, shape],
        name="regroup",
    )(where, x)


def gate_up_kernel(lay, where, x_ref, other_ref, gm, go, um, uo, up_ref, down_ref, keep_ref, own_ref, x_by, acc):
    rows = own_ref.shape[1]
    chips = lay.half // rows

    @pl.when(pl.program_id(0) == 0)
    def _():
        for e in range(lay.experts):
            x_by[e] = lay.of_expert(x_ref, e)
            x_by[lay.experts + e] = lay.of_expert(other_ref, e)

    for i, (wm, wo) in enumerate(((gm, go), (um, uo))):
        totals = []
        for e in range(lay.experts):
            total = dot(x_by[e], wm[e], 1, 0) + dot(x_by[lay.experts + e], wo[e], 1, 0)
            acc[i, e * lay.per:(e + 1) * lay.per, :] = total[:lay.per]
            totals.append(total)
        acc[i, lay.start:, :] = lay.tails(totals)
    at = functools.partial(chunk_rows, where, chips=chips, rows=rows)
    up_ref[0] = acc[0, at(2), :].astype(BF16)
    up_ref[1] = acc[1, at(1), :].astype(BF16)
    down_ref[0] = acc[1, at(2), :].astype(BF16)
    down_ref[1] = acc[0, at(chips - 1), :].astype(BF16)
    keep_ref[0] = acc[0, at(1), :]
    keep_ref[1] = acc[1, at(chips - 1), :]
    own_ref[0] = acc[0, at(0), :]
    own_ref[1] = acc[1, at(0), :]


def gate_up(where, x, other, gm, go, um, uo, lay, rows):
    experts, feats, width = gm.shape
    tile = 256
    weight = pl.BlockSpec((experts, feats, tile), lambda n, w: (0, 0, n))
    out = pl.BlockSpec((2, rows, tile), lambda n, w: (0, 0, n))
    shape = (2, rows, width)
    return pl.pallas_call(
        functools.partial(gate_up_kernel, lay),
        grid_spec=pltpu.PrefetchScalarGridSpec(
            num_scalar_prefetch=1,
            grid=(width // tile,),
            in_specs=[
                pl.BlockSpec(x.shape, lambda n, w: (0, 0)),
                pl.BlockSpec(other.shape, lambda n, w: (0, 0)),
                weight, weight, weight, weight,
            ],
            out_specs=[out, out, out, out],
            scratch_shapes=[
                pltpu.VMEM((2 * experts, lay.per + lay.tail, feats), BF16),
                pltpu.VMEM((2, lay.half, tile), F32),
            ],
        ),
        out_shape=[
            jax.ShapeDtypeStruct(shape, BF16),
            jax.ShapeDtypeStruct(shape, BF16),
            jax.ShapeDtypeStruct(shape, F32),
            jax.ShapeDtypeStruct(shape, F32),
        ],
        name="gate_up",
    )(where, x, other, gm, go, um, uo)


def hidden_grad_kernel(lay, where, g_ref, other_ref, dm, do, up_ref, down_ref, keep_ref, own_ref, g_by, acc):
    part = own_ref.shape[1]
    rows = 2 * part
    chips = lay.half // rows

    @pl.when(pl.program_id(0) == 0)
    def _():
        for e in range(lay.experts):
            g_by[e] = lay.of_expert(g_ref, e)
            g_by[lay.experts + e] = lay.of_expert(other_ref, e)

    totals = []
    for e in range(lay.experts):
        total = dot(g_by[e], dm[e], 1, 1) + dot(g_by[lay.experts + e], do[e], 1, 1)
        acc[e * lay.per:(e + 1) * lay.per, :] = total[:lay.per]
        totals.append(total)
    acc[lay.start:, :] = lay.tails(totals)

    def at(away, k):
        start = (where[0] + away) % chips * rows + k * part
        return acc[pl.ds(pl.multiple_of(start, 16), part), :]

    up_ref[0] = at(2, 0).astype(BF16)
    up_ref[1] = at(1, 1).astype(BF16)
    down_ref[0] = at(2, 1).astype(BF16)
    down_ref[1] = at(chips - 1, 0).astype(BF16)
    keep_ref[0] = at(1, 0)
    keep_ref[1] = at(chips - 1, 1)
    own_ref[0] = at(0, 0)
    own_ref[1] = at(0, 1)


def hidden_grad_parts(where, g, other, dm, do, lay, rows):
    experts, width, feats = dm.shape
    tile = 256
    weight = pl.BlockSpec((experts, tile, feats), lambda n, w: (0, n, 0))
    out = pl.BlockSpec((2, rows // 2, tile), lambda n, w: (0, 0, n))
    shape = (2, rows // 2, width)
    return pl.pallas_call(
        functools.partial(hidden_grad_kernel, lay),
        grid_spec=pltpu.PrefetchScalarGridSpec(
            num_scalar_prefetch=1,
            grid=(width // tile,),
            in_specs=[
                pl.BlockSpec(g.shape, lambda n, w: (0, 0)),
                pl.BlockSpec(other.shape, lambda n, w: (0, 0)),
                weight, weight,
            ],
            out_specs=[out, out, out, out],
            scratch_shapes=[
                pltpu.VMEM((2 * experts, lay.per + lay.tail, feats), BF16),
                pltpu.VMEM((lay.half, tile), F32),
            ],
        ),
        out_shape=[
            jax.ShapeDtypeStruct(shape, BF16),
            jax.ShapeDtypeStruct(shape, BF16),
            jax.ShapeDtypeStruct(shape, F32),
            jax.ShapeDtypeStruct(shape, F32),
        ],
        name="hidden_grad",
    )(where, g, other, dm, do)


def gather_rows(where, put_to, own, low, high, far, chips, rows):
    def put(away, value, skip=0):
        start = (where[0] + away) % chips * rows + skip
        put_to(pl.ds(pl.multiple_of(start, 16), value.shape[0]), value)

    put(0, own)
    put(chips - 1, low)
    put(1, high)
    skip = 0
    for value in far:
        put(2, value, skip)
        skip += value.shape[0]


def expert_out_kernel(lay, where, own, low, high, far_a, far_b, dm, do, mine_ref, other_ref, all_ref):
    rows = own.shape[0]

    def put_to(at, value):
        all_ref[at, :] = value

    gather_rows(where, put_to, own[...], low[...], high[...], (far_a[...], far_b[...]), lay.half // rows, rows)
    for out, weight, base in ((mine_ref, dm, where[1] * lay.blocks), (other_ref, do, 0)):
        totals = [dot(lay.of_expert(all_ref, e), weight[e], 1, 0).astype(BF16) for e in range(lay.experts)]
        lay.ungroup(totals, out, base)


def expert_out_of(where, pieces, dm, do, lay):
    experts, width, feats = dm.shape
    vmem = pl.BlockSpec(memory_space=pltpu.VMEM)
    block = (experts * lay.main + lay.tile, feats)
    full = jax.ShapeDtypeStruct((CORES * lay.blocks, *block), BF16)
    out = jax.ShapeDtypeStruct((lay.blocks, *block), BF16)
    return pl.pallas_call(
        functools.partial(expert_out_kernel, lay),
        in_specs=[pl.BlockSpec(memory_space=pltpu.SMEM)] + [vmem] * 7,
        out_specs=[vmem] * 3,
        out_shape=[full, out, jax.ShapeDtypeStruct((lay.half, width), BF16)],
        name="expert_out",
    )(where, *pieces, dm, do)


def slot_in_kernel(lay, where, own, low, high, far_g, far_u, gm, go, um, uo, mine_ref, other_ref, all_ref):
    rows = own.shape[1]
    for i, far in enumerate((far_g, far_u)):

        def put_to(at, value):
            all_ref[i, at, :] = value

        gather_rows(where, put_to, own[i], low[i], high[i], (far[...],), lay.half // rows, rows)
    for out, gw, uw, base in ((mine_ref, gm, um, where[1] * lay.blocks), (other_ref, go, uo, 0)):
        totals = []
        for e in range(lay.experts):
            total = dot(lay.of_expert(all_ref.at[0], e), gw[e], 1, 1)
            totals.append((total + dot(lay.of_expert(all_ref.at[1], e), uw[e], 1, 1)).astype(BF16))
        lay.ungroup(totals, out, base)


def slot_in_of(where, pieces, gm, go, um, uo, lay):
    experts, feats, width = gm.shape
    vmem = pl.BlockSpec(memory_space=pltpu.VMEM)
    block = (experts * lay.main + lay.tile, feats)
    full = jax.ShapeDtypeStruct((CORES * lay.blocks, *block), BF16)
    out = jax.ShapeDtypeStruct((lay.blocks, *block), BF16)
    return pl.pallas_call(
        functools.partial(slot_in_kernel, lay),
        in_specs=[pl.BlockSpec(memory_space=pltpu.SMEM)] + [vmem] * 9,
        out_specs=[vmem] * 3,
        out_shape=[full, out, jax.ShapeDtypeStruct((2, lay.half, width), BF16)],
        name="slot_in",
    )(where, *pieces, gm, go, um, uo)


def weight_grad_kernel(lay, count, a_own, a_far, b_own, b_far, *refs):
    outs, (a_by, b_by) = refs[:count], refs[count:]
    e = pl.program_id(0)
    main = pl.ds(pl.multiple_of(e * lay.per, 16), lay.per)
    at = [pl.ds(0, lay.per), pl.ds(lay.per, lay.per)]
    rest = [pl.ds(2 * lay.per, lay.tail), pl.ds(2 * lay.per + lay.tail, lay.tail)]

    @pl.when(pl.program_id(1) == 0)
    def _():
        for k, ref in enumerate((a_own, a_far)):
            a_by[:, at[k]] = ref[main, :].T
            tail = ref[lay.start:, :]
            a_by[:, rest[k]] = jnp.where(lay.tail_of(e), tail, jnp.zeros_like(tail)).T

    for i, out in enumerate(outs):
        for k, ref in enumerate((b_own, b_far)):
            b_by[at[k], :] = ref[i, main, :]
            b_by[rest[k], :] = ref[i, lay.start:, :]
        out[0] = dot(a_by[...], b_by[...], 1, 0).astype(BF16)


def weight_grad(a_own, a_far, b_own, b_far, lay):
    rows = 2 * (lay.per + lay.tail)
    a_cols, (count, _, b_cols) = a_own.shape[1], b_own.shape
    tile = 256
    a_spec = pl.BlockSpec(a_own.shape, lambda e, n: (0, 0))
    b_spec = pl.BlockSpec((count, lay.half, tile), lambda e, n: (0, 0, n))
    out = pl.BlockSpec((1, a_cols, tile), lambda e, n: (e, 0, n))
    return pl.pallas_call(
        functools.partial(weight_grad_kernel, lay, count),
        grid=(lay.experts, b_cols // tile),
        in_specs=[a_spec, a_spec, b_spec, b_spec],
        out_specs=[out] * count,
        out_shape=[jax.ShapeDtypeStruct((lay.experts, a_cols, b_cols), BF16)] * count,
        scratch_shapes=[pltpu.VMEM((a_cols, rows), BF16), pltpu.VMEM((rows, tile), BF16)],
        name="weight_grad",
    )(a_own, a_far, b_own, b_far)


def routing(ids, weight, owner, rank, allowed, block, experts_all):
    rows = ids.shape[0]
    experts = jnp.arange(experts_all, dtype=jnp.int32)
    hit = ids[:, :, None] == experts[None, None, :]
    member = jnp.any(hit, axis=1)
    t_row = lax.broadcasted_iota(jnp.int32, (rows, rows), 0)
    t_col = lax.broadcasted_iota(jnp.int32, (rows, rows), 1)
    earlier = ((t_col <= t_row) & (t_col // block == t_row // block)).astype(BF16)
    rank1 = jnp.where(member, dot(earlier, member.astype(BF16), 1, 0), 0.0)
    spread = (experts[:, None] == owner[None, :]).astype(BF16)
    rank1_s = dot(rank1.astype(BF16), spread, 1, 0)
    taken = rank1_s == (rank + 1).astype(F32)[None, :]
    if allowed is not None:
        taken = taken & allowed
    if weight is None:
        return taken.astype(BF16)
    weight_te = jnp.sum(jnp.where(hit, weight[:, :, None], 0.0), axis=1)
    weight_s = sum(dot(part, spread, 1, 0) for part in split3(weight_te))
    return taken.astype(BF16), jnp.where(taken, weight_s, 0.0)


def weighted_sum(weight_s, rows):
    return sum(dot(part, rows, 1, 0) for part in split3(weight_s))


def layer(tokens, out_grad, expert_ids, route_weight, gate_weight, up_weight, down_weight):
    n_y, n_z, n_x = (lax.axis_size(a) for a in ("y", "z_lo", "x"))
    n_cols = n_y * n_z * n_x
    n_reps = lax.axis_size("replica")
    tok_count, topk = expert_ids.shape
    local_experts, feats, _ = gate_weight.shape
    experts_all = local_experts * n_cols
    cap = tok_count * topk * 5 // (4 * experts_all)
    slots = experts_all * cap
    rows = slots // n_reps

    rep = lax.axis_index("replica")
    core = rep % CORES
    where = jnp.stack([rep // CORES, core]).astype(jnp.int32)
    to_swap = [(r, r ^ 1) for r in range(n_reps)]
    to_up = [(r, (r + CORES) % n_reps) for r in range(n_reps)]
    to_down = [(r, (r - CORES) % n_reps) for r in range(n_reps)]

    def swap(a):
        return lax.ppermute(a, "replica", to_swap)

    def up_one(a):
        return lax.ppermute(a, "replica", to_up)

    def down_one(a):
        return lax.ppermute(a, "replica", to_down)

    def tree_sum(send_up, send_down, keep, own):
        low = up_one(send_up)
        high = down_one(send_down)
        first = up_one((keep[0] + low[0].astype(F32)).astype(BF16))
        second = down_one((keep[1] + high[0].astype(F32)).astype(BF16))
        a = own[0] + high[1].astype(F32) + first.astype(F32)
        b = own[1] + low[1].astype(F32) + second.astype(F32)
        return a, b

    plane = n_y * n_x
    z_lo = lax.axis_index("z_lo")
    to_plane = [(z, n_z - 1 - z) for z in range(n_z)]
    lay = Rows(n_cols // CORES, local_experts, cap)

    def cross(a):
        return lax.ppermute(a, "z_lo", to_plane)

    def by_plane(mine, far):
        first = lax.select_n(z_lo == 0, far, mine)
        return jnp.concatenate([first, lax.select_n(z_lo == 0, mine, far)], axis=0)

    gate_other = swap(gate_weight)
    up_other = swap(up_weight)
    down_other = swap(down_weight)
    ids_other = cross(expert_ids)
    weight_other = cross(route_weight)
    out_grad_other = cross(out_grad)

    block_rows = local_experts * cap
    slot = jnp.arange(slots, dtype=jnp.int32)
    at, inner = slot // block_rows, slot % block_rows
    first = local_experts * lay.main
    which = jnp.where(inner < first, inner // lay.main, (inner - first) // lay.rest)
    rank = jnp.where(inner < first, inner % lay.main, lay.main + (inner - first) % lay.rest)

    def owner_of(z):
        return (((at // n_z // n_x) * n_z + z) * n_x + at // n_z % n_x) * local_experts + which

    picker = routing(expert_ids, None, owner_of(at % n_z), rank, None, tok_count, experts_all)
    send_x = dot(picker, tokens, 0, 0).astype(BF16)

    def exchange(a):
        a = a.reshape(n_cols, block_rows, feats)
        return lax.all_to_all(a, ("y", "x", "z_lo"), split_axis=0, concat_axis=0, tiled=True)

    def exchange_plane(a):
        a = a.reshape(plane, n_z * block_rows, feats)
        return lax.all_to_all(a, ("y", "x"), split_axis=0, concat_axis=0, tiled=True)

    def both_halves(mine, other):
        return lax.dynamic_update_slice_in_dim(mine, swap(other), (1 - core) * lay.blocks, 0)

    recv_x = exchange(send_x)
    x_keep, x_give = regroup(where, recv_x, lay)
    x_other = swap(x_give)

    token = jnp.arange(n_z * tok_count, dtype=jnp.int32)
    same = token[:, None] // tok_count == at[None, :] % n_z
    picker2, weight2 = routing(
        by_plane(expert_ids, ids_other), by_plane(route_weight, weight_other),
        owner_of(z_lo), rank, same, tok_count, experts_all)
    picked_g = dot(picker2, by_plane(out_grad, out_grad_other), 0, 0)
    send_g = (jnp.sum(weight2, axis=0)[:, None] * picked_g).astype(BF16)
    recv_g = exchange_plane(send_g).reshape(n_cols, block_rows, feats)

    gate, up = tree_sum(*gate_up(
        where, x_keep, x_other, gate_weight, gate_other, up_weight, up_other, lay, rows))

    g_keep, g_give = regroup(where, recv_g, lay)
    g_other = swap(g_give)
    grad_a, grad_b = tree_sum(*hidden_grad_parts(where, g_keep, g_other, down_weight, down_other, lay, rows))
    hidden_grad = jnp.concatenate([grad_a, grad_b], axis=0)

    own = (gate * jax.nn.sigmoid(gate) * up).astype(BF16)
    low, high = up_one(own), down_one(own)
    far_a, far_b = up_one(low[:rows // 2]), down_one(high[rows // 2:])
    mine, other, hidden = expert_out_of(
        where, (own, low, high, far_a, far_b), down_weight, down_other, lay)
    expert_out = both_halves(mine, other)
    returned = exchange_plane(expert_out).reshape(slots, feats)
    sums = weighted_sum(weight2, returned).reshape(n_z, tok_count, feats)
    sum_mine = lax.select_n(z_lo == 0, sums[1], sums[0])
    from_far = cross(lax.select_n(z_lo == 0, sums[0], sums[1]))

    gate, up = lax.optimization_barrier((gate, up))
    sig = jax.nn.sigmoid(gate)
    gate_grad = (hidden_grad * up * sig * (1.0 + gate * (1.0 - sig))).astype(BF16)
    up_grad = (hidden_grad * (gate * sig)).astype(BF16)
    own = jnp.stack([gate_grad, up_grad])
    low, high = up_one(own), down_one(own)
    far_g, far_u = up_one(low[0]), down_one(high[1])
    mine, other, grads = slot_in_of(
        where, (own, low, high, far_g, far_u), gate_weight, gate_other, up_weight, up_other, lay)
    slot_in = both_halves(mine, other)
    back_in = exchange(slot_in).reshape(slots, feats)
    in_grad = dot(picker, back_in, 1, 0).astype(BF16)

    hidden_other = swap(hidden)
    grad_down, = weight_grad(hidden, hidden_other, g_keep[None], g_give[None], lay)
    grads_other = swap(grads)
    grad_gate, grad_up = weight_grad(x_keep, x_give, grads, grads_other, lay)
    grad_up, sum_mine = lax.optimization_barrier((grad_up, sum_mine))
    mixed = (sum_mine + from_far).astype(BF16)
    return (mixed, in_grad, grad_gate, grad_up, grad_down)


def solution(mesh):
    n_y, n_z, n_x = 4, 2, 4
    devices = mesh.devices.reshape(n_y, n_z, n_x, mesh.shape["replica"])
    mesh = Mesh(devices, ("y", "z_lo", "x", "replica"))
    cols = ("y", "z_lo", "x")
    in_specs = (
        P(cols, "replica"),
        P(cols, "replica"),
        P(cols, None),
        P(cols, None),
        P(cols, "replica", None),
        P(cols, "replica", None),
        P(cols, None, "replica"),
    )
    out_specs = (
        P(cols, "replica"),
        P(cols, "replica"),
        P(cols, "replica", None),
        P(cols, "replica", None),
        P(cols, None, "replica"),
    )
    return jax.shard_map(layer, mesh=mesh, in_specs=in_specs, out_specs=out_specs, check_vma=False)
```

```python
import functools
import jax
import jax.numpy as jnp
from jax import lax
from jax.experimental import pallas as pl
from jax.experimental.pallas import tpu as pltpu
from jax.sharding import Mesh, PartitionSpec as P


F32 = jnp.float32
BF16 = jnp.bfloat16
CORES = 2


def dot(a, b, ca, cb):
    return lax.dot_general(a, b, (((ca,), (cb,)), ((), ())), preferred_element_type=F32)


def split3(w):
    hi = w.astype(BF16)
    rest = w - hi.astype(F32)
    mid = rest.astype(BF16)
    low = (rest - mid.astype(F32)).astype(BF16)
    return hi, mid, low


def chunk_rows(where, away, chips, rows):
    return pl.ds(pl.multiple_of((where[0] + away) % chips * rows, 16), rows)


class Rows:
    def __init__(self, blocks, experts, cap):
        self.blocks, self.experts = blocks, experts
        self.main = cap // 8 * 8
        self.rest = cap - self.main
        self.tile = experts * self.rest
        self.per = blocks * self.main
        self.tail = blocks * self.tile
        self.start = experts * self.per
        self.half = self.start + self.tail

    def tail_of(self, e):
        row = lax.broadcasted_iota(jnp.int32, (self.tail, 1), 0)
        return row % self.tile // self.rest == e

    def of_expert(self, ref, e):
        return jnp.concatenate([ref[e * self.per:(e + 1) * self.per, :], ref[self.start:, :]], axis=0)

    def tails(self, totals):
        out = totals[0][self.per:]
        for e in range(1, self.experts):
            out = jnp.where(self.tail_of(e), totals[e][self.per:], out)
        return out

    def regroup(self, read, out):
        for j in range(self.blocks):
            for e in range(self.experts):
                out[e * self.per + j * self.main:e * self.per + (j + 1) * self.main, :] = (
                    read(j)[e * self.main:(e + 1) * self.main, :])
        first = self.experts * self.main
        for j in range(0, self.blocks, 2):
            pair = jnp.concatenate([read(j)[first:, :], read(j + 1)[first:, :]], axis=0)
            out[self.start + j * self.tile:self.start + (j + 2) * self.tile, :] = pair

    def ungroup(self, totals, out, base):
        tails = self.tails(totals)
        first = self.experts * self.main
        for j in range(self.blocks):
            for e in range(self.experts):
                out[base + j, e * self.main:(e + 1) * self.main, :] = totals[e][j * self.main:(j + 1) * self.main]
            out[base + j, first:, :] = tails[j * self.tile:(j + 1) * self.tile]


def regroup_kernel(lay, where, x_ref, keep_ref, give_ref):
    for out, core in ((keep_ref, where[1]), (give_ref, 1 - where[1])):
        lay.regroup(lambda j: x_ref[core * lay.blocks + j], out)


def regroup(where, x, lay):
    vmem = pl.BlockSpec(memory_space=pltpu.VMEM)
    shape = jax.ShapeDtypeStruct((lay.half, x.shape[2]), BF16)
    return pl.pallas_call(
        functools.partial(regroup_kernel, lay),
        in_specs=[pl.BlockSpec(memory_space=pltpu.SMEM), vmem],
        out_specs=[vmem, vmem],
        out_shape=[shape, shape],
        name="regroup",
    )(where, x)


def gate_up_kernel(lay, where, x_ref, other_ref, gm, go, um, uo, up_ref, down_ref, keep_ref, own_ref, x_by, acc):
    rows = own_ref.shape[1]
    chips = lay.half // rows

    @pl.when(pl.program_id(0) == 0)
    def _():
        for e in range(lay.experts):
            x_by[e] = lay.of_expert(x_ref, e)
            x_by[lay.experts + e] = lay.of_expert(other_ref, e)

    for i, (wm, wo) in enumerate(((gm, go), (um, uo))):
        totals = []
        for e in range(lay.experts):
            total = dot(x_by[e], wm[e], 1, 0) + dot(x_by[lay.experts + e], wo[e], 1, 0)
            acc[i, e * lay.per:(e + 1) * lay.per, :] = total[:lay.per]
            totals.append(total)
        acc[i, lay.start:, :] = lay.tails(totals)
    at = functools.partial(chunk_rows, where, chips=chips, rows=rows)
    up_ref[0] = acc[0, at(2), :].astype(BF16)
    up_ref[1] = acc[1, at(1), :].astype(BF16)
    down_ref[0] = acc[1, at(2), :].astype(BF16)
    down_ref[1] = acc[0, at(chips - 1), :].astype(BF16)
    keep_ref[0] = acc[0, at(1), :]
    keep_ref[1] = acc[1, at(chips - 1), :]
    own_ref[0] = acc[0, at(0), :]
    own_ref[1] = acc[1, at(0), :]


def gate_up(where, x, other, gm, go, um, uo, lay, rows):
    experts, feats, width = gm.shape
    tile = 256
    weight = pl.BlockSpec((experts, feats, tile), lambda n, w: (0, 0, n))
    out = pl.BlockSpec((2, rows, tile), lambda n, w: (0, 0, n))
    shape = (2, rows, width)
    return pl.pallas_call(
        functools.partial(gate_up_kernel, lay),
        grid_spec=pltpu.PrefetchScalarGridSpec(
            num_scalar_prefetch=1,
            grid=(width // tile,),
            in_specs=[
                pl.BlockSpec(x.shape, lambda n, w: (0, 0)),
                pl.BlockSpec(other.shape, lambda n, w: (0, 0)),
                weight, weight, weight, weight,
            ],
            out_specs=[out, out, out, out],
            scratch_shapes=[
                pltpu.VMEM((2 * experts, lay.per + lay.tail, feats), BF16),
                pltpu.VMEM((2, lay.half, tile), F32),
            ],
        ),
        out_shape=[
            jax.ShapeDtypeStruct(shape, BF16),
            jax.ShapeDtypeStruct(shape, BF16),
            jax.ShapeDtypeStruct(shape, F32),
            jax.ShapeDtypeStruct(shape, F32),
        ],
        name="gate_up",
    )(where, x, other, gm, go, um, uo)


def hidden_grad_kernel(lay, where, g_ref, other_ref, dm, do, up_ref, down_ref, keep_ref, own_ref, g_by, acc):
    part = own_ref.shape[1]
    rows = 2 * part
    chips = lay.half // rows

    @pl.when(pl.program_id(0) == 0)
    def _():
        for e in range(lay.experts):
            g_by[e] = lay.of_expert(g_ref, e)
            g_by[lay.experts + e] = lay.of_expert(other_ref, e)

    totals = []
    for e in range(lay.experts):
        total = dot(g_by[e], dm[e], 1, 1) + dot(g_by[lay.experts + e], do[e], 1, 1)
        acc[e * lay.per:(e + 1) * lay.per, :] = total[:lay.per]
        totals.append(total)
    acc[lay.start:, :] = lay.tails(totals)

    def at(away, k):
        start = (where[0] + away) % chips * rows + k * part
        return acc[pl.ds(pl.multiple_of(start, 16), part), :]

    up_ref[0] = at(2, 0).astype(BF16)
    up_ref[1] = at(1, 1).astype(BF16)
    down_ref[0] = at(2, 1).astype(BF16)
    down_ref[1] = at(chips - 1, 0).astype(BF16)
    keep_ref[0] = at(1, 0)
    keep_ref[1] = at(chips - 1, 1)
    own_ref[0] = at(0, 0)
    own_ref[1] = at(0, 1)


def hidden_grad_parts(where, g, other, dm, do, lay, rows):
    experts, width, feats = dm.shape
    tile = 256
    weight = pl.BlockSpec((experts, tile, feats), lambda n, w: (0, n, 0))
    out = pl.BlockSpec((2, rows // 2, tile), lambda n, w: (0, 0, n))
    shape = (2, rows // 2, width)
    return pl.pallas_call(
        functools.partial(hidden_grad_kernel, lay),
        grid_spec=pltpu.PrefetchScalarGridSpec(
            num_scalar_prefetch=1,
            grid=(width // tile,),
            in_specs=[
                pl.BlockSpec(g.shape, lambda n, w: (0, 0)),
                pl.BlockSpec(other.shape, lambda n, w: (0, 0)),
                weight, weight,
            ],
            out_specs=[out, out, out, out],
            scratch_shapes=[
                pltpu.VMEM((2 * experts, lay.per + lay.tail, feats), BF16),
                pltpu.VMEM((lay.half, tile), F32),
            ],
        ),
        out_shape=[
            jax.ShapeDtypeStruct(shape, BF16),
            jax.ShapeDtypeStruct(shape, BF16),
            jax.ShapeDtypeStruct(shape, F32),
            jax.ShapeDtypeStruct(shape, F32),
        ],
        name="hidden_grad",
    )(where, g, other, dm, do)


def gather_rows(where, put_to, own, low, high, far, chips, rows):
    def put(away, value, skip=0):
        start = (where[0] + away) % chips * rows + skip
        put_to(pl.ds(pl.multiple_of(start, 16), value.shape[0]), value)

    put(0, own)
    put(chips - 1, low)
    put(1, high)
    skip = 0
    for value in far:
        put(2, value, skip)
        skip += value.shape[0]


def expert_out_kernel(lay, where, own, low, high, far_a, far_b, dm, do, mine_ref, other_ref, all_ref):
    rows = own.shape[0]

    def put_to(at, value):
        all_ref[at, :] = value

    gather_rows(where, put_to, own[...], low[...], high[...], (far_a[...], far_b[...]), lay.half // rows, rows)
    for out, weight, base in ((mine_ref, dm, where[1] * lay.blocks), (other_ref, do, 0)):
        totals = [dot(lay.of_expert(all_ref, e), weight[e], 1, 0).astype(BF16) for e in range(lay.experts)]
        lay.ungroup(totals, out, base)


def expert_out_of(where, pieces, dm, do, lay):
    experts, width, feats = dm.shape
    vmem = pl.BlockSpec(memory_space=pltpu.VMEM)
    block = (experts * lay.main + lay.tile, feats)
    full = jax.ShapeDtypeStruct((CORES * lay.blocks, *block), BF16)
    out = jax.ShapeDtypeStruct((lay.blocks, *block), BF16)
    return pl.pallas_call(
        functools.partial(expert_out_kernel, lay),
        in_specs=[pl.BlockSpec(memory_space=pltpu.SMEM)] + [vmem] * 7,
        out_specs=[vmem] * 3,
        out_shape=[full, out, jax.ShapeDtypeStruct((lay.half, width), BF16)],
        name="expert_out",
    )(where, *pieces, dm, do)


def slot_in_kernel(lay, where, own, low, high, far_g, far_u, gm, go, um, uo, mine_ref, other_ref, all_ref):
    rows = own.shape[1]
    for i, far in enumerate((far_g, far_u)):

        def put_to(at, value):
            all_ref[i, at, :] = value

        gather_rows(where, put_to, own[i], low[i], high[i], (far[...],), lay.half // rows, rows)
    for out, gw, uw, base in ((mine_ref, gm, um, where[1] * lay.blocks), (other_ref, go, uo, 0)):
        totals = []
        for e in range(lay.experts):
            total = dot(lay.of_expert(all_ref.at[0], e), gw[e], 1, 1)
            totals.append((total + dot(lay.of_expert(all_ref.at[1], e), uw[e], 1, 1)).astype(BF16))
        lay.ungroup(totals, out, base)


def slot_in_of(where, pieces, gm, go, um, uo, lay):
    experts, feats, width = gm.shape
    vmem = pl.BlockSpec(memory_space=pltpu.VMEM)
    block = (experts * lay.main + lay.tile, feats)
    full = jax.ShapeDtypeStruct((CORES * lay.blocks, *block), BF16)
    out = jax.ShapeDtypeStruct((lay.blocks, *block), BF16)
    return pl.pallas_call(
        functools.partial(slot_in_kernel, lay),
        in_specs=[pl.BlockSpec(memory_space=pltpu.SMEM)] + [vmem] * 9,
        out_specs=[vmem] * 3,
        out_shape=[full, out, jax.ShapeDtypeStruct((2, lay.half, width), BF16)],
        name="slot_in",
    )(where, *pieces, gm, go, um, uo)


def weight_grad_kernel(lay, count, a_own, a_far, b_own, b_far, *refs):
    outs, (a_by, b_by) = refs[:count], refs[count:]
    e = pl.program_id(0)
    main = pl.ds(pl.multiple_of(e * lay.per, 16), lay.per)
    at = [pl.ds(0, lay.per), pl.ds(lay.per, lay.per)]
    rest = [pl.ds(2 * lay.per, lay.tail), pl.ds(2 * lay.per + lay.tail, lay.tail)]

    @pl.when(pl.program_id(1) == 0)
    def _():
        for k, ref in enumerate((a_own, a_far)):
            a_by[:, at[k]] = ref[main, :].T
            tail = ref[lay.start:, :]
            a_by[:, rest[k]] = jnp.where(lay.tail_of(e), tail, jnp.zeros_like(tail)).T

    for i, out in enumerate(outs):
        for k, ref in enumerate((b_own, b_far)):
            b_by[at[k], :] = ref[i, main, :]
            b_by[rest[k], :] = ref[i, lay.start:, :]
        out[0] = dot(a_by[...], b_by[...], 1, 0).astype(BF16)


def weight_grad(a_own, a_far, b_own, b_far, lay):
    rows = 2 * (lay.per + lay.tail)
    a_cols, (count, _, b_cols) = a_own.shape[1], b_own.shape
    tile = 256
    a_spec = pl.BlockSpec(a_own.shape, lambda e, n: (0, 0))
    b_spec = pl.BlockSpec((count, lay.half, tile), lambda e, n: (0, 0, n))
    out = pl.BlockSpec((1, a_cols, tile), lambda e, n: (e, 0, n))
    return pl.pallas_call(
        functools.partial(weight_grad_kernel, lay, count),
        grid=(lay.experts, b_cols // tile),
        in_specs=[a_spec, a_spec, b_spec, b_spec],
        out_specs=[out] * count,
        out_shape=[jax.ShapeDtypeStruct((lay.experts, a_cols, b_cols), BF16)] * count,
        scratch_shapes=[pltpu.VMEM((a_cols, rows), BF16), pltpu.VMEM((rows, tile), BF16)],
        name="weight_grad",
    )(a_own, a_far, b_own, b_far)


def routing(ids, weight, owner, rank, allowed, block, experts_all):
    rows = ids.shape[0]
    experts = jnp.arange(experts_all, dtype=jnp.int32)
    hit = ids[:, :, None] == experts[None, None, :]
    member = jnp.any(hit, axis=1)
    t_row = lax.broadcasted_iota(jnp.int32, (rows, rows), 0)
    t_col = lax.broadcasted_iota(jnp.int32, (rows, rows), 1)
    earlier = ((t_col <= t_row) & (t_col // block == t_row // block)).astype(BF16)
    rank1 = jnp.where(member, dot(earlier, member.astype(BF16), 1, 0), 0.0)
    spread = (experts[:, None] == owner[None, :]).astype(BF16)
    rank1_s = dot(rank1.astype(BF16), spread, 1, 0)
    taken = rank1_s == (rank + 1).astype(F32)[None, :]
    if allowed is not None:
        taken = taken & allowed
    if weight is None:
        return taken.astype(BF16)
    weight_te = jnp.sum(jnp.where(hit, weight[:, :, None], 0.0), axis=1)
    weight_s = sum(dot(part, spread, 1, 0) for part in split3(weight_te))
    return taken.astype(BF16), jnp.where(taken, weight_s, 0.0)


def weighted_sum(weight_s, rows):
    return sum(dot(part, rows, 1, 0) for part in split3(weight_s))


def layer(tokens, out_grad, expert_ids, route_weight, gate_weight, up_weight, down_weight):
    n_y, n_z, n_x = (lax.axis_size(a) for a in ("y", "z_lo", "x"))
    n_cols = n_y * n_z * n_x
    n_reps = lax.axis_size("replica")
    tok_count, topk = expert_ids.shape
    local_experts, feats, _ = gate_weight.shape
    experts_all = local_experts * n_cols
    cap = tok_count * topk * 5 // (4 * experts_all)
    slots = experts_all * cap
    rows = slots // n_reps

    rep = lax.axis_index("replica")
    core = rep % CORES
    where = jnp.stack([rep // CORES, core]).astype(jnp.int32)
    to_swap = [(r, r ^ 1) for r in range(n_reps)]
    to_up = [(r, (r + CORES) % n_reps) for r in range(n_reps)]
    to_down = [(r, (r - CORES) % n_reps) for r in range(n_reps)]

    def swap(a):
        return lax.ppermute(a, "replica", to_swap)

    def up_one(a):
        return lax.ppermute(a, "replica", to_up)

    def down_one(a):
        return lax.ppermute(a, "replica", to_down)

    def tree_sum(send_up, send_down, keep, own):
        low = up_one(send_up)
        high = down_one(send_down)
        first = up_one((keep[0] + low[0].astype(F32)).astype(BF16))
        second = down_one((keep[1] + high[0].astype(F32)).astype(BF16))
        a = own[0] + high[1].astype(F32) + first.astype(F32)
        b = own[1] + low[1].astype(F32) + second.astype(F32)
        return a, b

    plane = n_y * n_x
    z_lo = lax.axis_index("z_lo")
    to_plane = [(z, n_z - 1 - z) for z in range(n_z)]
    lay = Rows(n_cols // CORES, local_experts, cap)

    def cross(a):
        return lax.ppermute(a, "z_lo", to_plane)

    def by_plane(mine, far):
        first = lax.select_n(z_lo == 0, far, mine)
        return jnp.concatenate([first, lax.select_n(z_lo == 0, mine, far)], axis=0)

    gate_other = swap(gate_weight)
    up_other = swap(up_weight)
    down_other = swap(down_weight)
    ids_other = cross(expert_ids)
    weight_other = cross(route_weight)
    out_grad_other = cross(out_grad)

    block_rows = local_experts * cap
    slot = jnp.arange(slots, dtype=jnp.int32)
    at, inner = slot // block_rows, slot % block_rows
    first = local_experts * lay.main
    which = jnp.where(inner < first, inner // lay.main, (inner - first) // lay.rest)
    rank = jnp.where(inner < first, inner % lay.main, lay.main + (inner - first) % lay.rest)

    def owner_of(z):
        return (((at // n_z // n_x) * n_z + z) * n_x + at // n_z % n_x) * local_experts + which

    picker = routing(expert_ids, None, owner_of(at % n_z), rank, None, tok_count, experts_all)
    send_x = dot(picker, tokens, 0, 0).astype(BF16)

    def exchange(a):
        a = a.reshape(n_cols, block_rows, feats)
        return lax.all_to_all(a, ("y", "x", "z_lo"), split_axis=0, concat_axis=0, tiled=True)

    def exchange_plane(a):
        a = a.reshape(plane, n_z * block_rows, feats)
        return lax.all_to_all(a, ("y", "x"), split_axis=0, concat_axis=0, tiled=True)

    def both_halves(mine, other):
        return lax.dynamic_update_slice_in_dim(mine, swap(other), (1 - core) * lay.blocks, 0)

    recv_x = exchange(send_x)
    x_keep, x_give = regroup(where, recv_x, lay)
    x_other = swap(x_give)

    token = jnp.arange(n_z * tok_count, dtype=jnp.int32)
    same = token[:, None] // tok_count == at[None, :] % n_z
    picker2, weight2 = routing(
        by_plane(expert_ids, ids_other), by_plane(route_weight, weight_other),
        owner_of(z_lo), rank, same, tok_count, experts_all)
    picked_g = dot(picker2, by_plane(out_grad, out_grad_other), 0, 0)
    send_g = (jnp.sum(weight2, axis=0)[:, None] * picked_g).astype(BF16)
    recv_g = exchange_plane(send_g).reshape(n_cols, block_rows, feats)

    gate, up = tree_sum(*gate_up(
        where, x_keep, x_other, gate_weight, gate_other, up_weight, up_other, lay, rows))

    g_keep, g_give = regroup(where, recv_g, lay)
    g_other = swap(g_give)
    grad_a, grad_b = tree_sum(*hidden_grad_parts(where, g_keep, g_other, down_weight, down_other, lay, rows))
    hidden_grad = jnp.concatenate([grad_a, grad_b], axis=0)

    own = (gate * jax.nn.sigmoid(gate) * up).astype(BF16)
    low, high = up_one(own), down_one(own)
    far_a, far_b = up_one(low[:rows // 2]), down_one(high[rows // 2:])
    mine, other, hidden = expert_out_of(
        where, (own, low, high, far_a, far_b), down_weight, down_other, lay)
    expert_out = both_halves(mine, other)
    returned = exchange_plane(expert_out).reshape(slots, feats)
    first, second = weight2[:tok_count], weight2[tok_count:]
    weight_mine = lax.select_n(z_lo == 0, second, first)
    weight_far = lax.select_n(z_lo == 0, first, second)
    weight_mine, weight_far = lax.optimization_barrier((weight_mine, weight_far))
    from_far = cross(weighted_sum(weight_far, returned))
    sum_mine = weighted_sum(weight_mine, returned)

    gate, up = lax.optimization_barrier((gate, up))
    sig = jax.nn.sigmoid(gate)
    gate_grad = (hidden_grad * up * sig * (1.0 + gate * (1.0 - sig))).astype(BF16)
    up_grad = (hidden_grad * (gate * sig)).astype(BF16)
    own = jnp.stack([gate_grad, up_grad])
    low, high = up_one(own), down_one(own)
    far_g, far_u = up_one(low[0]), down_one(high[1])
    mine, other, grads = slot_in_of(
        where, (own, low, high, far_g, far_u), gate_weight, gate_other, up_weight, up_other, lay)
    slot_in = both_halves(mine, other)
    back_in = exchange(slot_in).reshape(slots, feats)
    in_grad = dot(picker, back_in, 1, 0).astype(BF16)

    hidden_other = swap(hidden)
    grad_down, = weight_grad(hidden, hidden_other, g_keep[None], g_give[None], lay)
    grads_other = swap(grads)
    grad_gate, grad_up = weight_grad(x_keep, x_give, grads, grads_other, lay)
    grad_up, sum_mine = lax.optimization_barrier((grad_up, sum_mine))
    mixed = (sum_mine + from_far).astype(BF16)
    return (mixed, in_grad, grad_gate, grad_up, grad_down)


def solution(mesh):
    n_y, n_z, n_x = 4, 2, 4
    devices = mesh.devices.reshape(n_y, n_z, n_x, mesh.shape["replica"])
    mesh = Mesh(devices, ("y", "z_lo", "x", "replica"))
    cols = ("y", "z_lo", "x")
    in_specs = (
        P(cols, "replica"),
        P(cols, "replica"),
        P(cols, None),
        P(cols, None),
        P(cols, "replica", None),
        P(cols, "replica", None),
        P(cols, None, "replica"),
    )
    out_specs = (
        P(cols, "replica"),
        P(cols, "replica"),
        P(cols, "replica", None),
        P(cols, "replica", None),
        P(cols, None, "replica"),
    )
    return jax.shard_map(layer, mesh=mesh, in_specs=in_specs, out_specs=out_specs, check_vma=False)
```
